32 devices in a mesh: groups: 2 (over x), ctx: 16 (over z, y, core).
Axes of the slice: x: 2, y: 2, z: 4, core: 2. Of those that a mesh axis runs over, the one named last changes fastest.
Arguments:
- gate_out: bfloat16 [8192, 2048], P(('groups', 'ctx')), parts along dimension 0, may hold values from -6 to 6
- gate_in: bfloat16 [8192, 2048], P(('groups', 'ctx')), parts along dimension 0, may hold values from -6 to 6
- values: bfloat16 [8192, 2048], P(('groups', 'ctx')), parts along dimension 0, may hold values from -6 to 6
- filter_taps: bfloat16 [1024, 2048], P(None, 'ctx'), may hold values from -0.1875 to 0.1875
- skip_gain: float32 [2048], replicated, may hold values from -4 to 4
Outputs:
- operator_out: bfloat16 [8192, 2048], P(('groups', 'ctx')), parts along dimension 0
The draws below stay inside these ranges and needn't reach their ends.
There are 2 independent parts, one for each index of `groups`. The reference program is written for one: setup_inputs(seed, part) draws one part's arguments, and reference() takes and returns one part's arrays. A program takes and returns all parts, laid end to end along the dimension named above; an argument that names none is the same for every part. Nothing has to cross between parts.
All inputs are finite; a program needn't handle non-finite values.
Results may differ from the reference program's by a relative error of at most 0.005.
Values may be sent and summed in bfloat16 or wider, within the bound.
No kernel may reach another device: no remote copies, remote signals or barrier semaphores. Data moves between devices by JAX's collectives and lax.ppermute only.
A program may use at most 128 MiB of HBM per device.

```python
import jax
import jax.numpy as jnp

D = 2048
TAPS = 1024
LENGTH = 4096


def level_of(key, extent, cuts, smallest, largest):
    def one(position, blocks):
        steps = jax.random.uniform(jax.random.fold_in(jax.random.fold_in(key, 6), position), (blocks,), jnp.float32, smallest / len(cuts), largest / len(cuts))
        return jnp.repeat(jnp.exp(steps), extent[position] // blocks).reshape((-1,) + (1,) * (len(extent) - position - 1))

    level = one(*cuts[0])
    for cut in cuts[1:]:
        level = level * one(*cut)
    return level


def gaussian(stream_key, shape, scale, most, split=(), held_as=jnp.bfloat16):
    drawn = scale * jax.random.normal(stream_key, shape, jnp.float32)
    if split:
        drawn = drawn * level_of(stream_key, shape, split, -0.22, 0.18)
    return jnp.clip(drawn, -most, most).astype(held_as)


def setup_inputs(seed: int = 0, part: int = 0) -> dict:
    streams_of = jax.random.split(jax.random.key(seed), 6)
    own_keys = jax.random.split(jax.random.fold_in(streams_of[5], part), 6)
    gate_out = gaussian(own_keys[0], (LENGTH, D), 1.0, 6.0, ((0, 16),))
    gate_in = gaussian(own_keys[1], (LENGTH, D), 1.0, 6.0, ((0, 16),))
    values = gaussian(own_keys[2], (LENGTH, D), 1.0, 6.0, ((0, 16),))
    filter_taps = gaussian(streams_of[3], (TAPS, D), TAPS ** -0.5, 0.1875, ((1, 16),))
    skip_gain = gaussian(streams_of[4], (D,), 1.0, 4.0, (), jnp.float32)
    return {"gate_out": gate_out, "gate_in": gate_in, "values": values, "filter_taps": filter_taps, "skip_gain": skip_gain}


def reference(gate_out, gate_in, values, filter_taps, skip_gain):
    product = (gate_in.astype(jnp.float32) * values.astype(jnp.float32)).astype(jnp.bfloat16)
    length = product.shape[0]
    taps = filter_taps.shape[0]
    signal = product.astype(jnp.float32)
    padded_taps = jnp.concatenate([filter_taps.astype(jnp.float32), jnp.zeros((length - taps, filter_taps.shape[1]), jnp.float32)], axis=0)
    spectrum_prod = jnp.fft.rfft(signal, axis=0) * jnp.fft.rfft(padded_taps, axis=0)
    convolved = jnp.fft.irfft(spectrum_prod, n=length, axis=0).astype(signal.dtype)
    mixed = gate_out.astype(jnp.float32) * (convolved + skip_gain[None, :] * signal)
    return mixed.astype(jnp.bfloat16)
```

```python
import functools

import jax
import jax.numpy as jnp
import ml_dtypes
import numpy as np
from jax import lax
from jax.experimental import pallas as pl
from jax.experimental.pallas import tpu as pltpu
from jax.sharding import PartitionSpec as P

LANES = 128
BF16 = jnp.bfloat16
F32 = jnp.float32


def two_parts(table):
    high = table.astype(ml_dtypes.bfloat16)
    low = (table - high.astype(np.float64)).astype(ml_dtypes.bfloat16)
    return high, low


def bin_order(rows):
    return np.concatenate([np.arange(0, rows, 2), np.arange(1, rows, 2)])


def forward_tables(rows):
    bins = bin_order(rows)[:, None] + 0.5
    angle = bins * np.arange(rows)[None, :] * (np.pi / rows)
    return two_parts(np.concatenate([np.cos(angle), -np.sin(angle)], axis=0))


def inverse_tables(rows):
    bins = bin_order(rows)[None, :] + 0.5
    angle = bins * (np.arange(rows)[:, None] + rows) * (np.pi / rows)
    return two_parts(np.concatenate([np.cos(angle), -np.sin(angle)], axis=1) / rows)


def matmul(a, b):
    return jnp.dot(a, b, preferred_element_type=F32)


def scalar_spec():
    return pl.BlockSpec(memory_space=pltpu.SMEM)


def params():
    return pltpu.CompilerParams(vmem_limit_bytes=56 << 20)


def product_kernel(layers, members, where_ref, gate_ref, values_ref, *piece_refs):
    member = where_ref[0]
    for apart in range(members):
        held = member ^ apart
        for layer in range(layers):
            lanes = pl.ds(pl.multiple_of((layer * members + held) * LANES, LANES), LANES)
            gated = gate_ref[:, lanes].astype(F32) * values_ref[:, lanes].astype(F32)
            piece_refs[apart][:, layer * LANES : (layer + 1) * LANES] = gated.astype(BF16)


def product_pieces(where, gate_in, values, layers, members):
    rows, channels = values.shape
    width = channels // (layers * members)
    held = channels // members
    if width != LANES:
        product = (gate_in.astype(F32) * values.astype(F32)).astype(BF16)
        product = product.reshape(rows, layers, members, width).transpose(2, 0, 1, 3)
        product = product.reshape(members, rows, held)
        return [lax.dynamic_index_in_dim(product, where[0] ^ d, 0, False) for d in range(members)]
    step = rows // 4
    return pl.pallas_call(
        functools.partial(product_kernel, layers, members),
        grid=(4,),
        in_specs=[scalar_spec()] + [pl.BlockSpec((step, channels), lambda r: (r, 0))] * 2,
        out_specs=[pl.BlockSpec((step, held), lambda r: (r, 0))] * members,
        out_shape=[jax.ShapeDtypeStruct((rows, held), BF16)] * members,
        compiler_params=params(),
        cost_estimate=pl.CostEstimate(
            flops=rows * channels, bytes_accessed=rows * channels * 6, transcendentals=0
        ),
    )(where, gate_in, values)


def taps_kernel(layers, where_ref, high_ref, low_ref, own_ref, *refs):
    count = layers - 1
    near_refs, far_refs, (out_ref, taps) = refs[:count], refs[count : 2 * count], refs[2 * count :]
    layer, group = where_ref[1], where_ref[2]
    rows = high_ref.shape[1]
    half = near_refs[0].shape[0]
    near = pl.ds(pl.multiple_of(group * half, half), half)
    far = pl.ds(pl.multiple_of((1 - group) * half, half), half)
    taps[:, pl.ds(pl.multiple_of(layer * LANES, LANES), LANES)] = own_ref[...]
    for apart in range(1, layers):
        source = lax.rem(layer + layers - apart, layers)
        lanes = pl.ds(pl.multiple_of(source * LANES, LANES), LANES)
        taps[near, lanes] = near_refs[apart - 1][...]
        taps[far, lanes] = far_refs[apart - 1][...]
    for lag in range(out_ref.shape[0]):
        block = taps[lag * rows : (lag + 1) * rows]
        out_ref[lag] = matmul(high_ref[...], block) + matmul(low_ref[...], block)


def plain_taps_kernel(high_ref, low_ref, taps_ref, out_ref):
    rows = high_ref.shape[1]
    for lag in range(out_ref.shape[0]):
        block = taps_ref[lag * rows : (lag + 1) * rows]
        out_ref[lag] = matmul(high_ref[...], block) + matmul(low_ref[...], block)


def own_kernel(members, where_ref, high_ref, low_ref, *refs):
    block_refs, out_ref = refs[:members], refs[members]
    member = where_ref[0]
    for apart in range(members):
        block = block_refs[apart][...]
        out_ref[member ^ apart] = matmul(high_ref[...], block) + matmul(low_ref[...], block)


def own_spectra(where, tables, blocks):
    members = len(blocks)
    rows, held = blocks[0].shape
    chunk = min(256, held)
    whole = pl.BlockSpec((2 * rows, rows), lambda c: (0, 0))
    return pl.pallas_call(
        functools.partial(own_kernel, members),
        grid=(held // chunk,),
        in_specs=[scalar_spec(), whole, whole]
        + [pl.BlockSpec((rows, chunk), lambda c: (0, c))] * members,
        out_specs=pl.BlockSpec((members, 2 * rows, chunk), lambda c: (0, 0, c)),
        out_shape=jax.ShapeDtypeStruct((members, 2 * rows, held), F32),
        compiler_params=params(),
        cost_estimate=pl.CostEstimate(
            flops=members * 8 * rows * rows * held,
            bytes_accessed=members * rows * held * 10,
            transcendentals=0,
        ),
    )(where, *tables, *blocks)


def mix_kernel(
    members, where_ref, high_ref, low_ref, back_high_ref, back_low_ref, skip_ref, taps_ref, own_ref, *refs
):
    halo_refs, block_refs = refs[:members], refs[members : 2 * members]
    out_refs, (halo, sums) = refs[2 * members : 3 * members], refs[3 * members :]
    member = where_ref[0]
    rows = high_ref.shape[1]
    for apart in range(members):
        block = halo_refs[apart][...]
        halo[member ^ apart] = matmul(high_ref[...], block) + matmul(low_ref[...], block)

    def spectrum(position, at):
        source = halo if position < 0 else own_ref
        return source[position % members, pl.ds(at, 8), :], source[position % members, pl.ds(at + rows, 8), :]

    def one(at, sign):
        blocks = [spectrum(position, at) for position in range(-members, members)]
        windows = []
        for (before_real, before_imag), (real, imag) in zip(blocks, blocks[1:]):
            if sign > 0:
                windows.append((before_real + imag, before_imag - real))
            else:
                windows.append((before_real - imag, before_imag + real))
        taps = [
            (taps_ref[lag, pl.ds(at, 8), :], taps_ref[lag, pl.ds(at + rows, 8), :])
            for lag in range(members)
        ]
        for output in range(members):
            real_sum, imag_sum = None, None
            for lag in range(members):
                real, imag = windows[members - 1 + output - lag]
                tap_real, tap_imag = taps[lag]
                real_part = tap_real * real - tap_imag * imag
                imag_part = tap_real * imag + tap_imag * real
                real_sum = real_part if real_sum is None else real_sum + real_part
                imag_sum = imag_part if imag_sum is None else imag_sum + imag_part
            sums[output, pl.ds(at, 8), :] = real_sum
            sums[output, pl.ds(at + rows, 8), :] = imag_sum

    count = rows // 16

    @pl.loop(0, count)
    def _(step):
        one(pl.multiple_of(step * 8, 8), 1)

    @pl.loop(count, 2 * count)
    def _(step):
        one(pl.multiple_of(step * 8, 8), -1)

    for apart in range(members):
        total = sums[member ^ apart]
        high = total.astype(BF16)
        low = (total - high.astype(F32)).astype(BF16)
        convolved = matmul(back_high_ref[...], high) + (
            matmul(back_high_ref[...], low) + matmul(back_low_ref[...], high)
        )
        mixed = convolved + skip_ref[...] * block_refs[apart][...].astype(F32)
        out_refs[apart][...] = mixed.astype(BF16)


def mixed_pieces(where, tables, back_tables, skip, taps, own, halo, blocks):
    members = len(blocks)
    rows, held = blocks[0].shape
    chunk = min(256, held)
    forward = pl.BlockSpec((2 * rows, rows), lambda c: (0, 0))
    backward = pl.BlockSpec((rows, 2 * rows), lambda c: (0, 0))
    spectra = pl.BlockSpec((members, 2 * rows, chunk), lambda c: (0, 0, c))
    piece = pl.BlockSpec((rows, chunk), lambda c: (0, c))
    return pl.pallas_call(
        functools.partial(mix_kernel, members),
        grid=(held // chunk,),
        in_specs=[scalar_spec(), forward, forward, backward, backward]
        + [pl.BlockSpec((1, chunk), lambda c: (0, c)), spectra, spectra]
        + [piece] * (2 * members),
        out_specs=[piece] * members,
        out_shape=[jax.ShapeDtypeStruct((rows, held), BF16)] * members,
        scratch_shapes=[pltpu.VMEM((members, 2 * rows, chunk), F32)] * 2,
        compiler_params=params(),
        cost_estimate=pl.CostEstimate(
            flops=members * 20 * rows * rows * held,
            bytes_accessed=members * rows * held * 22,
            transcendentals=0,
        ),
    )(where, *tables, *back_tables, skip, taps, own, *halo, *blocks)


def gate_kernel(layers, members, where_ref, gate_ref, *refs):
    piece_refs, out_ref = refs[:members], refs[members]
    member = where_ref[0]
    for apart in range(members):
        held = member ^ apart
        for layer in range(layers):
            lanes = pl.ds(pl.multiple_of((layer * members + held) * LANES, LANES), LANES)
            mixed = piece_refs[apart][:, layer * LANES : (layer + 1) * LANES].astype(F32)
            out_ref[:, lanes] = (gate_ref[:, lanes].astype(F32) * mixed).astype(BF16)


def gated_output(where, gate_out, pieces, layers, members):
    rows, channels = gate_out.shape
    held = channels // members
    width = held // layers
    if width != LANES:
        stacked = jnp.stack(pieces)
        stacked = jnp.stack(
            [lax.dynamic_index_in_dim(stacked, where[0] ^ d, 0, False) for d in range(members)]
        )
        mixed = stacked.reshape(members, rows, layers, width).transpose(1, 2, 0, 3)
        mixed = mixed.reshape(rows, channels).astype(F32)
        return (gate_out.astype(F32) * mixed).astype(BF16)
    step = rows // 4
    return pl.pallas_call(
        functools.partial(gate_kernel, layers, members),
        grid=(4,),
        in_specs=[scalar_spec(), pl.BlockSpec((step, channels), lambda r: (r, 0))]
        + [pl.BlockSpec((step, held), lambda r: (r, 0))] * members,
        out_specs=pl.BlockSpec((step, channels), lambda r: (r, 0)),
        out_shape=jax.ShapeDtypeStruct((rows, channels), BF16),
        compiler_params=params(),
    )(where, gate_out, *pieces)


def tap_spectra(where, tables, filter_taps, layers, members, groups):
    count, width = filter_taps.shape
    rows = tables[0].shape[1]
    held = width * layers
    length = layers * members
    out_shape = jax.ShapeDtypeStruct((count // rows, 2 * rows, held), F32)
    cost = pl.CostEstimate(
        flops=8 * count * rows * held, bytes_accessed=count * held * 10, transcendentals=0
    )
    if width != LANES or groups != 2:
        ring = [[layer * members + member for layer in range(layers)] for member in range(members)]
        taps = lax.all_gather(filter_taps, "ctx", axis=1, tiled=True, axis_index_groups=ring)
        return pl.pallas_call(
            plain_taps_kernel, out_shape=out_shape, compiler_params=params(), cost_estimate=cost
        )(*tables, taps)
    half = lax.dynamic_slice_in_dim(filter_taps, where[2] * (count // 2), count // 2, 0)
    near = [
        lax.ppermute(half, "ctx", [(i, (i + apart * members) % length) for i in range(length)])
        for apart in range(1, layers)
    ]
    far = [lax.ppermute(part, "groups", [(0, 1), (1, 0)]) for part in near]
    return pl.pallas_call(
        functools.partial(taps_kernel, layers),
        in_specs=[scalar_spec()] + [pl.BlockSpec(memory_space=pltpu.VMEM)] * (2 * layers + 1),
        out_specs=pl.BlockSpec(memory_space=pltpu.VMEM),
        out_shape=out_shape,
        scratch_shapes=[pltpu.VMEM((count, held), BF16)],
        compiler_params=params(),
        cost_estimate=cost,
    )(where, *tables, filter_taps, *near, *far)


def on_device(gate_out, gate_in, values, filter_taps, skip_gain):
    rows, channels = values.shape
    length = lax.axis_size("ctx")
    members = filter_taps.shape[0] // rows
    layers = length // members
    width = channels // length
    index = lax.axis_index("ctx")
    where = jnp.stack([index % members, index // members, lax.axis_index("groups")]).astype(jnp.int32)
    tables = [jnp.asarray(t) for t in forward_tables(rows)]
    back_tables = [jnp.asarray(t) for t in inverse_tables(rows)]

    def to_member(value, apart, ahead):
        pairs = [
            (i, (i // members + ahead) % layers * members + (i % members ^ apart))
            for i in range(length)
        ]
        return lax.ppermute(value, "ctx", pairs)

    pieces = product_pieces(where, gate_in, values, layers, members)
    halo = [to_member(pieces[d], d, 1) for d in range(members)]
    blocks = [pieces[0]] + [to_member(pieces[d], d, 0) for d in range(1, members)]
    taps = tap_spectra(where, tables, filter_taps, layers, members, lax.axis_size("groups"))
    own = own_spectra(where, tables, blocks)
    skip = skip_gain.reshape(layers, members, width)
    skip = lax.dynamic_index_in_dim(skip, where[0], 1, False).reshape(1, layers * width)
    mixed = mixed_pieces(where, tables, back_tables, skip, taps, own, halo, blocks)
    mixed = [mixed[0]] + [to_member(mixed[d], d, 0) for d in range(1, members)]
    return gated_output(where, gate_out, mixed, layers, members)


def solution(mesh):
    in_specs = (
        P(("groups", "ctx"), None),
        P(("groups", "ctx"), None),
        P(("groups", "ctx"), None),
        P(None, "ctx"),
        P(),
    )
    out_specs = P(("groups", "ctx"), None)
    return jax.shard_map(
        on_device, mesh=mesh, in_specs=in_specs, out_specs=out_specs, check_vma=False
    )
```

```python
import functools

import jax
import jax.numpy as jnp
import ml_dtypes
import numpy as np
from jax import lax
from jax.experimental import pallas as pl
from jax.experimental.pallas import tpu as pltpu
from jax.sharding import PartitionSpec as P

LANES = 128
CHUNKS = 2
BF16 = jnp.bfloat16
F32 = jnp.float32
VMEM = pl.BlockSpec(memory_space=pltpu.VMEM)
SMALL = pl.CostEstimate(flops=1000, bytes_accessed=1000, transcendentals=0)


def two_parts(table):
    high = table.astype(ml_dtypes.bfloat16)
    low = (table - high.astype(np.float64)).astype(ml_dtypes.bfloat16)
    return jnp.asarray(high), jnp.asarray(low)


def bin_order(rows):
    return np.concatenate([np.arange(0, rows, 2), np.arange(1, rows, 2)])


def forward_tables(rows):
    bins = bin_order(rows)[:, None] + 0.5
    angle = bins * np.arange(rows)[None, :] * (np.pi / rows)
    return two_parts(np.concatenate([np.cos(angle), -np.sin(angle)], axis=0))


def inverse_tables(rows):
    bins = bin_order(rows)[None, :] + 0.5
    angle = bins * (np.arange(rows)[:, None] + rows) * (np.pi / rows)
    return two_parts(np.concatenate([np.cos(angle), -np.sin(angle)], axis=1) / rows)


def matmul(a, b):
    return jnp.dot(a, b, preferred_element_type=F32)


def params(mib):
    return pltpu.CompilerParams(vmem_limit_bytes=mib << 20)


def place(members):
    index = lax.axis_index("ctx")
    return lax.rem(index, members), lax.div(index, members)


def aligned(position, size):
    return pl.ds(pl.multiple_of(position * size, size), size)


def product_kernel(
    layers, members, gate_hbm, values_hbm, half_ref, keep_same_ref, keep_other_ref, *more
):
    del half_ref
    send_refs, (gate, values, sems) = more[:-3], more[-3:]
    member, _ = place(members)
    per_chunk = layers // CHUNKS
    count = sems.shape[1]
    step = gate.shape[0] // count

    def copies(index):
        rows = slice(index * step, (index + 1) * step)
        return [
            pltpu.make_async_copy(source.at[rows], target.at[rows], sems.at[which, index])
            for which, (source, target) in enumerate(((gate_hbm, gate), (values_hbm, values)))
        ]

    for index in range(count):
        for copy in copies(index):
            copy.start()
    refs = [
        lambda chunk, rows, lanes: keep_same_ref.at[chunk, rows, lanes],
        lambda chunk, rows, lanes: send_refs[2 * chunk].at[rows, lanes],
        lambda chunk, rows, lanes: keep_other_ref.at[chunk, rows, lanes],
        lambda chunk, rows, lanes: send_refs[2 * chunk + 1].at[rows, lanes],
    ]
    for index in range(count):
        rows = slice(index * step, (index + 1) * step)
        for copy in copies(index):
            copy.wait()
        for apart in range(members):
            held = member ^ apart
            for layer in range(layers):
                lanes = aligned(layer * members + held, LANES)
                gated = gate[rows, lanes].astype(F32) * values[rows, lanes].astype(F32)
                at = layer % per_chunk * LANES
                target = refs[apart](layer // per_chunk, rows, slice(at, at + LANES))
                target[...] = gated.astype(BF16)


def product_pieces(gate_in, values, half, layers, members):
    rows, channels = values.shape
    width = channels // (layers * members)
    chunk = channels // members // CHUNKS
    if width != LANES:
        member, _ = place(members)
        product = (gate_in.astype(F32) * values.astype(F32)).astype(BF16)
        product = product.reshape(rows, CHUNKS, layers // CHUNKS, members, width)
        product = product.transpose(3, 1, 0, 2, 4).reshape(members, CHUNKS, rows, chunk)
        pieces = [lax.dynamic_index_in_dim(product, member ^ d, 0, False) for d in range(members)]
        return pieces[0], pieces[2], pieces[1][0], pieces[3][0], pieces[1][1], pieces[3][1]
    count = 4
    there = pl.BlockSpec(memory_space=pltpu.HBM)
    return pl.pallas_call(
        functools.partial(product_kernel, layers, members),
        in_specs=[there, there, pl.BlockSpec(memory_space=pl.ANY)],
        out_specs=[VMEM] * (2 + 2 * CHUNKS),
        out_shape=[jax.ShapeDtypeStruct((CHUNKS, rows, chunk), BF16)] * 2
        + [jax.ShapeDtypeStruct((rows, chunk), BF16)] * (2 * CHUNKS),
        scratch_shapes=[pltpu.VMEM((rows, channels), BF16)] * 2 + [pltpu.SemaphoreType.DMA((2, count))],
        compiler_params=params(8),
        cost_estimate=SMALL,
    )(gate_in, values, half)


def pack_kernel(same_ref, other_ref, *refs):
    core_refs, (mine_ref, across_ref, *beyond_refs) = refs[: 2 * CHUNKS], refs[2 * CHUNKS :]
    for part in range(CHUNKS):
        mine_ref[part, 0] = same_ref[part]
        mine_ref[part, 1] = core_refs[2 * part][...]
        for target in (across_ref.at[part], beyond_refs[part]):
            target[0] = other_ref[part]
            target[1] = core_refs[2 * part + 1][...]


def payloads(same, other, core):
    _, rows, chunk = same.shape
    return pl.pallas_call(
        pack_kernel,
        in_specs=[VMEM] * (2 + len(core)),
        out_specs=[VMEM] * (2 + CHUNKS),
        out_shape=[jax.ShapeDtypeStruct((CHUNKS, 2, rows, chunk), BF16)] * 2
        + [jax.ShapeDtypeStruct((2, rows, chunk), BF16)] * CHUNKS,
        compiler_params=params(8),
        cost_estimate=SMALL,
    )(same, other, *core)


def join_kernel(*refs):
    at = 0
    for ref in refs[:-1]:
        count = ref.shape[0]
        refs[-1][at : at + count] = ref[...]
        at += count


def joined(pieces):
    return pl.pallas_call(
        join_kernel,
        in_specs=[VMEM] * len(pieces),
        out_specs=VMEM,
        out_shape=jax.ShapeDtypeStruct((sum(p.shape[0] for p in pieces), *pieces[0].shape[1:]), BF16),
        compiler_params=params(8),
        cost_estimate=SMALL,
    )(*pieces)


def put_tap_spectra(high_ref, low_ref, taps, out_ref):
    rows = high_ref.shape[1]
    chunk = out_ref.shape[-1]
    for part in range(CHUNKS):
        for lag in range(out_ref.shape[1]):
            block = taps[lag * rows : (lag + 1) * rows, part * chunk : (part + 1) * chunk]
            out_ref[part, lag] = matmul(high_ref[...], block) + matmul(low_ref[...], block)


def taps_kernel(layers, members, high_ref, low_ref, own_ref, near_ref, far_ref, out_ref, taps):
    _, layer = place(members)
    group = lax.axis_index("groups")
    half = near_ref.shape[1]
    near, far = aligned(group, half), aligned(1 - group, half)
    taps[:, aligned(layer, LANES)] = own_ref[...]
    for apart in range(1, layers):
        lanes = aligned(layer ^ apart, LANES)
        at = (None, 0, 2, 1)[apart]
        taps[near, lanes] = near_ref[at]
        taps[far, lanes] = far_ref[at]
    put_tap_spectra(high_ref, low_ref, taps, out_ref)


def near_half(filter_taps, layers, groups):
    count, width = filter_taps.shape
    if width != LANES or groups != 2 or layers != 4:
        return None
    start = lax.axis_index("groups") * (count // 2)
    return lax.dynamic_slice_in_dim(filter_taps, start, count // 2, 0)[None]


def tap_spectra(tables, filter_taps, near, layers, members):
    count, width = filter_taps.shape
    rows = tables[0].shape[1]
    held = width * layers
    out_shape = jax.ShapeDtypeStruct((CHUNKS, count // rows, 2 * rows, held // CHUNKS), F32)
    if near is None:
        ring = [[layer * members + member for layer in range(layers)] for member in range(members)]
        taps = lax.all_gather(filter_taps, "ctx", axis=1, tiled=True, axis_index_groups=ring)
        return pl.pallas_call(
            put_tap_spectra,
            in_specs=[VMEM] * 3,
            out_specs=VMEM,
            out_shape=out_shape,
            compiler_params=params(20),
            cost_estimate=SMALL,
        )(*tables, taps)
    far = lax.ppermute(near, "groups", [(0, 1), (1, 0)])
    return pl.pallas_call(
        functools.partial(taps_kernel, layers, members),
        in_specs=[VMEM] * 5,
        out_specs=VMEM,
        out_shape=out_shape,
        scratch_shapes=[pltpu.VMEM((count, held), BF16)],
        compiler_params=params(20),
        cost_estimate=SMALL,
    )(*tables, filter_taps, near, far)


def window(before, after, sign):
    (before_real, before_imag), (real, imag) = before, after
    if sign > 0:
        return before_real + imag, before_imag - real
    return before_real - imag, before_imag + real


def sum_products(pairs):
    real_sum = imag_sum = None
    for (tap_real, tap_imag), (real, imag) in pairs:
        real_part = tap_real * real - tap_imag * imag
        imag_part = tap_real * imag + tap_imag * real
        real_sum = real_part if real_sum is None else real_sum + real_part
        imag_sum = imag_part if imag_sum is None else imag_sum + imag_part
    return real_sum, imag_sum


def for_bins(rows, step, body):
    count = rows // (2 * step)
    for sign, first in ((1, 0), (-1, count)):

        @pl.loop(first, first + count)
        def _(index):
            body(pl.multiple_of(index * step, step), sign)


def reader(ref, rows, at, step):
    def read(*index):
        return ref[*index, pl.ds(at, step), :], ref[*index, pl.ds(at + rows, step), :]

    return read


def own_kernel(
    members, high_ref, low_ref, taps_ref, mine_ref, across_ref, part_ref, first_ref, spectra
):
    member, _ = place(members)
    rows = high_ref.shape[1]
    for part in range(CHUNKS):
        blocks = [mine_ref[part, 0], mine_ref[part, 1], across_ref[part, 0], across_ref[part, 1]]
        for apart, block in enumerate(blocks):
            spectra[member ^ apart] = matmul(high_ref[...], block) + matmul(low_ref[...], block)
        first_ref[part] = spectra[0]

        def body(at, sign):
            read = reader(spectra, rows, at, 8)
            taps_read = reader(taps_ref, rows, at, 8)
            taps = [taps_read(part, lag) for lag in range(members - 1)]
            blocks = [read(position) for position in range(members)]
            windows = [window(a, b, sign) for a, b in zip(blocks, blocks[1:])]
            for output in range(1, members):
                total = sum_products([(taps[lag], windows[output - 1 - lag]) for lag in range(output)])
                part_ref[part, output - 1, pl.ds(at, 8), :] = total[0]
                part_ref[part, output - 1, pl.ds(at + rows, 8), :] = total[1]

        for_bins(rows, 8, body)


def own_partials(tables, taps, mine, across):
    members = taps.shape[1]
    chunk = taps.shape[-1]
    rows = tables[0].shape[1]
    return pl.pallas_call(
        functools.partial(own_kernel, members),
        in_specs=[VMEM] * 5,
        out_specs=[VMEM] * 2,
        out_shape=[
            jax.ShapeDtypeStruct((CHUNKS, members - 1, 2 * rows, chunk), F32),
            jax.ShapeDtypeStruct((CHUNKS, 2 * rows, chunk), F32),
        ],
        scratch_shapes=[pltpu.VMEM((members, 2 * rows, chunk), F32)],
        compiler_params=params(20),
        cost_estimate=SMALL,
    )(*tables, taps, mine, across)


def mix_kernel(
    members,
    part,
    high_ref,
    low_ref,
    back_high_ref,
    back_low_ref,
    skip_ref,
    taps_ref,
    part_ref,
    first_ref,
    mine_ref,
    across_ref,
    ahead_ref,
    beyond_ref,
    *refs,
):
    out_refs, (halo, sums) = refs[:members], refs[members:]
    member, _ = place(members)
    rows = high_ref.shape[1]
    halo_blocks = [ahead_ref[part, 0], ahead_ref[part, 1], beyond_ref[0], beyond_ref[1]]
    for apart, block in enumerate(halo_blocks):
        halo[member ^ apart] = matmul(high_ref[...], block) + matmul(low_ref[...], block)

    def body(at, sign):
        read = reader(halo, rows, at, 8)
        taps_read = reader(taps_ref, rows, at, 8)
        taps = [taps_read(part, lag) for lag in range(members)]
        blocks = [read(position) for position in range(members)]
        blocks.append(reader(first_ref, rows, at, 8)(part))
        windows = [window(a, b, sign) for a, b in zip(blocks, blocks[1:])]
        for output in range(members):
            total = sum_products(
                [(taps[lag], windows[members - 1 + output - lag]) for lag in range(output, members)]
            )
            if output:
                before = reader(part_ref, rows, at, 8)(part, output - 1)
                total = total[0] + before[0], total[1] + before[1]
            sums[output, pl.ds(at, 8), :] = total[0]
            sums[output, pl.ds(at + rows, 8), :] = total[1]

    for_bins(rows, 8, body)
    blocks = [mine_ref[part, 0], mine_ref[part, 1], across_ref[part, 0], across_ref[part, 1]]
    for apart, block in enumerate(blocks):
        total = sums[member ^ apart]
        high = total.astype(BF16)
        low = (total - high.astype(F32)).astype(BF16)
        convolved = matmul(back_high_ref[...], high) + (
            matmul(back_high_ref[...], low) + matmul(back_low_ref[...], high)
        )
        mixed = convolved + skip_ref[part] * block.astype(F32)
        out_refs[apart][...] = mixed.astype(BF16)


def mixed_pieces(part, tables, back_tables, skip, taps, partial, first, *blocks):
    members, chunk = taps.shape[1], taps.shape[-1]
    rows = tables[0].shape[1]
    return pl.pallas_call(
        functools.partial(mix_kernel, members, part),
        in_specs=[VMEM] * 12,
        out_specs=[VMEM] * members,
        out_shape=[jax.ShapeDtypeStruct((rows, chunk), BF16)] * members,
        scratch_shapes=[pltpu.VMEM((members, 2 * rows, chunk), F32)] * 2,
        compiler_params=params(20),
        cost_estimate=SMALL,
    )(*tables, *back_tables, skip, taps, partial, first, *blocks)


def gate_kernel(layers, members, part, gate_ref, *refs):
    piece_refs, out_ref = refs[:members], refs[-1]
    member, _ = place(members)
    for apart in range(members):
        held = member ^ apart
        for layer in range(layers):
            lanes = aligned(layer * members + held, LANES)
            mixed = piece_refs[apart][:, layer * LANES : (layer + 1) * LANES].astype(F32)
            out_ref[:, lanes] = (gate_ref[:, lanes].astype(F32) * mixed).astype(BF16)


def gated_output(part, gate_out, pieces, layers, members, out):
    rows, channels = gate_out.shape
    chunk = channels // members // CHUNKS
    width = channels // (layers * members)
    wide = channels // CHUNKS
    if width != LANES:
        member, _ = place(members)
        stacked = jnp.stack(pieces)
        stacked = jnp.stack(
            [lax.dynamic_index_in_dim(stacked, member ^ d, 0, False) for d in range(members)]
        )
        mixed = stacked.reshape(members, rows, layers // CHUNKS, width).transpose(1, 2, 0, 3)
        gate = gate_out[:, part * wide : (part + 1) * wide].astype(F32)
        gated = (gate * mixed.reshape(rows, wide).astype(F32)).astype(BF16)
        return gated if out is None else jnp.concatenate([out, gated], axis=1)
    step = rows // 2
    there = pl.BlockSpec((step, wide), lambda r: (r, part))
    more = [] if out is None else [out]
    return pl.pallas_call(
        functools.partial(gate_kernel, layers // CHUNKS, members, part),
        grid=(2,),
        in_specs=[there]
        + [pl.BlockSpec((step, chunk), lambda r: (r, 0))] * members
        + [pl.BlockSpec(memory_space=pl.ANY)] * len(more),
        out_specs=there,
        out_shape=jax.ShapeDtypeStruct((rows, channels), BF16),
        input_output_aliases={members + 1: 0} if more else {},
        compiler_params=params(16),
        cost_estimate=SMALL,
    )(gate_out, *pieces, *more)


def on_device(gate_out, gate_in, values, filter_taps, skip_gain):
    rows, channels = values.shape
    length = lax.axis_size("ctx")
    members = filter_taps.shape[0] // rows
    layers = length // members
    width = channels // length
    member, _ = place(members)
    tables, back_tables = forward_tables(rows), inverse_tables(rows)

    def to_member(value, apart, ahead):
        pairs = [
            (i, (i // members + ahead) % layers * members + (i % members ^ apart))
            for i in range(length)
        ]
        return lax.ppermute(value, "ctx", pairs)

    def to_layer(value, apart):
        pairs = [(i, (i // members ^ apart) * members + i % members) for i in range(length)]
        return lax.ppermute(value, "ctx", pairs)

    half = near_half(filter_taps, layers, lax.axis_size("groups"))
    near = None
    if half is not None:
        two_away = to_layer(half, 2)
    same, other, *send = product_pieces(gate_in, values, half, layers, members)
    core = [to_member(piece, 1, 0) for piece in send]
    if half is not None:
        two_away, core = lax.optimization_barrier((two_away, core))
    mine, to_across, *to_beyond = payloads(same, other, core)
    if half is not None:
        one_and_three_away = to_layer(joined([half, two_away]), 1)
        near = joined([one_and_three_away, two_away])
    ahead = to_member(mine, 0, 1)
    beyond = [to_member(piece, 2, 1) for piece in to_beyond]
    across = to_member(to_across, 2, 0)
    taps = tap_spectra(tables, filter_taps, near, layers, members)
    partial, first = own_partials(tables, taps, mine, across)
    skip = skip_gain.reshape(layers, members, width)
    skip = lax.dynamic_index_in_dim(skip, member, 1, False).reshape(CHUNKS, 1, channels // members // CHUNKS)
    out = None
    for part in range(CHUNKS):
        mixed = mixed_pieces(
            part, tables, back_tables, skip, taps, partial, first, mine, across, ahead, beyond[part]
        )
        mixed = [mixed[0]] + [to_member(mixed[d], d, 0) for d in range(1, members)]
        out = gated_output(part, gate_out, mixed, layers, members, out)
    return out


def solution(mesh):
    in_specs = (
        P(("groups", "ctx"), None),
        P(("groups", "ctx"), None),
        P(("groups", "ctx"), None),
        P(None, "ctx"),
        P(),
    )
    out_specs = P(("groups", "ctx"), None)
    return jax.shard_map(
        on_device, mesh=mesh, in_specs=in_specs, out_specs=out_specs, check_vma=False
    )
```

```python
import functools

import jax
import jax.numpy as jnp
import ml_dtypes
import numpy as np
from jax import lax
from jax.experimental import pallas as pl
from jax.experimental.pallas import tpu as pltpu
from jax.sharding import PartitionSpec as P

LANES = 128
CHUNKS = 2
BF16 = jnp.bfloat16
F32 = jnp.float32
VMEM = pl.BlockSpec(memory_space=pltpu.VMEM)
SMALL = pl.CostEstimate(flops=1000, bytes_accessed=1000, transcendentals=0)


def two_parts(table):
    high = table.astype(ml_dtypes.bfloat16)
    low = (table - high.astype(np.float64)).astype(ml_dtypes.bfloat16)
    return jnp.asarray(high), jnp.asarray(low)


def bin_order(rows):
    return np.concatenate([np.arange(0, rows, 2), np.arange(1, rows, 2)])


def forward_tables(rows):
    bins = bin_order(rows)[:, None] + 0.5
    angle = bins * np.arange(rows)[None, :] * (np.pi / rows)
    return two_parts(np.concatenate([np.cos(angle), -np.sin(angle)], axis=0))


def inverse_tables(rows):
    bins = bin_order(rows)[None, :] + 0.5
    angle = bins * (np.arange(rows)[:, None] + rows) * (np.pi / rows)
    return two_parts(np.concatenate([np.cos(angle), -np.sin(angle)], axis=1) / rows)


def matmul(a, b):
    return jnp.dot(a, b, preferred_element_type=F32)


def params(mib):
    return pltpu.CompilerParams(vmem_limit_bytes=mib << 20)


def place(members):
    index = lax.axis_index("ctx")
    return lax.rem(index, members), lax.div(index, members)


def aligned(position, size):
    return pl.ds(pl.multiple_of(position * size, size), size)


def product_kernel(
    layers, members, gate_hbm, values_hbm, half_ref, keep_same_ref, keep_other_ref, *more
):
    del half_ref
    send_refs, (gate, values, sems) = more[:-3], more[-3:]
    member, _ = place(members)
    per_chunk = layers // CHUNKS
    count = sems.shape[1]
    step = gate.shape[0] // count

    def copies(index):
        rows = slice(index * step, (index + 1) * step)
        return [
            pltpu.make_async_copy(source.at[rows], target.at[rows], sems.at[which, index])
            for which, (source, target) in enumerate(((gate_hbm, gate), (values_hbm, values)))
        ]

    for index in range(count):
        for copy in copies(index):
            copy.start()
    refs = [
        lambda chunk, rows, lanes: keep_same_ref.at[chunk, rows, lanes],
        lambda chunk, rows, lanes: send_refs[2 * chunk].at[rows, lanes],
        lambda chunk, rows, lanes: keep_other_ref.at[chunk, rows, lanes],
        lambda chunk, rows, lanes: send_refs[2 * chunk + 1].at[rows, lanes],
    ]
    for index in range(count):
        rows = slice(index * step, (index + 1) * step)
        for copy in copies(index):
            copy.wait()
        for apart in range(members):
            held = member ^ apart
            for layer in range(layers):
                lanes = aligned(layer * members + held, LANES)
                gated = gate[rows, lanes].astype(F32) * values[rows, lanes].astype(F32)
                at = layer % per_chunk * LANES
                target = refs[apart](layer // per_chunk, rows, slice(at, at + LANES))
                target[...] = gated.astype(BF16)


def product_pieces(gate_in, values, half, layers, members):
    rows, channels = values.shape
    width = channels // (layers * members)
    chunk = channels // members // CHUNKS
    if width != LANES:
        member, _ = place(members)
        product = (gate_in.astype(F32) * values.astype(F32)).astype(BF16)
        product = product.reshape(rows, CHUNKS, layers // CHUNKS, members, width)
        product = product.transpose(3, 1, 0, 2, 4).reshape(members, CHUNKS, rows, chunk)
        pieces = [lax.dynamic_index_in_dim(product, member ^ d, 0, False) for d in range(members)]
        return pieces[0], pieces[2], pieces[1][0], pieces[3][0], pieces[1][1], pieces[3][1]
    count = 4
    there = pl.BlockSpec(memory_space=pltpu.HBM)
    return pl.pallas_call(
        functools.partial(product_kernel, layers, members),
        in_specs=[there, there, pl.BlockSpec(memory_space=pl.ANY)],
        out_specs=[VMEM] * (2 + 2 * CHUNKS),
        out_shape=[jax.ShapeDtypeStruct((CHUNKS, rows, chunk), BF16)] * 2
        + [jax.ShapeDtypeStruct((rows, chunk), BF16)] * (2 * CHUNKS),
        scratch_shapes=[pltpu.VMEM((rows, channels), BF16)] * 2 + [pltpu.SemaphoreType.DMA((2, count))],
        compiler_params=params(8),
        cost_estimate=SMALL,
    )(*(pltpu.with_memory_space_constraint(x, pltpu.HBM) for x in (gate_in, values)), half)


def pack_kernel(same_ref, other_ref, *refs):
    core_refs, (mine_ref, across_ref, *beyond_refs) = refs[: 2 * CHUNKS], refs[2 * CHUNKS :]
    for part in range(CHUNKS):
        mine_ref[part, 0] = same_ref[part]
        mine_ref[part, 1] = core_refs[2 * part][...]
        for target in (across_ref.at[part], beyond_refs[part]):
            target[0] = other_ref[part]
            target[1] = core_refs[2 * part + 1][...]


def payloads(same, other, core):
    _, rows, chunk = same.shape
    return pl.pallas_call(
        pack_kernel,
        in_specs=[VMEM] * (2 + len(core)),
        out_specs=[VMEM] * (2 + CHUNKS),
        out_shape=[jax.ShapeDtypeStruct((CHUNKS, 2, rows, chunk), BF16)] * 2
        + [jax.ShapeDtypeStruct((2, rows, chunk), BF16)] * CHUNKS,
        compiler_params=params(8),
        cost_estimate=SMALL,
    )(same, other, *core)


def join_kernel(*refs):
    at = 0
    for ref in refs[:-1]:
        count = ref.shape[0]
        refs[-1][at : at + count] = ref[...]
        at += count


def joined(pieces):
    return pl.pallas_call(
        join_kernel,
        in_specs=[VMEM] * len(pieces),
        out_specs=VMEM,
        out_shape=jax.ShapeDtypeStruct((sum(p.shape[0] for p in pieces), *pieces[0].shape[1:]), BF16),
        compiler_params=params(8),
        cost_estimate=SMALL,
    )(*pieces)


def put_tap_spectra(high_ref, low_ref, taps, out_ref):
    rows = high_ref.shape[1]
    chunk = out_ref.shape[-1]
    for part in range(CHUNKS):
        for lag in range(out_ref.shape[1]):
            block = taps[lag * rows : (lag + 1) * rows, part * chunk : (part + 1) * chunk]
            out_ref[part, lag] = matmul(high_ref[...], block) + matmul(low_ref[...], block)


def taps_kernel(layers, members, high_ref, low_ref, own_ref, near_ref, far_ref, out_ref, taps):
    _, layer = place(members)
    group = lax.axis_index("groups")
    half = near_ref.shape[1]
    near, far = aligned(group, half), aligned(1 - group, half)
    taps[:, aligned(layer, LANES)] = own_ref[...]
    for apart in range(1, layers):
        lanes = aligned(layer ^ apart, LANES)
        taps[near, lanes] = near_ref[apart - 1]
        taps[far, lanes] = far_ref[apart - 1]
    put_tap_spectra(high_ref, low_ref, taps, out_ref)


def near_half(filter_taps, layers, groups):
    count, width = filter_taps.shape
    if width != LANES or groups != 2 or layers != 4:
        return None
    start = lax.axis_index("groups") * (count // 2)
    return lax.dynamic_slice_in_dim(filter_taps, start, count // 2, 0)[None]


def tap_spectra(tables, filter_taps, near, layers, members):
    count, width = filter_taps.shape
    rows = tables[0].shape[1]
    held = width * layers
    out_shape = jax.ShapeDtypeStruct((CHUNKS, count // rows, 2 * rows, held // CHUNKS), F32)
    if near is None:
        ring = [[layer * members + member for layer in range(layers)] for member in range(members)]
        taps = lax.all_gather(filter_taps, "ctx", axis=1, tiled=True, axis_index_groups=ring)
        return pl.pallas_call(
            put_tap_spectra,
            in_specs=[VMEM] * 3,
            out_specs=VMEM,
            out_shape=out_shape,
            compiler_params=params(20),
            cost_estimate=SMALL,
        )(*tables, taps)
    far = lax.ppermute(near, "groups", [(0, 1), (1, 0)])
    return pl.pallas_call(
        functools.partial(taps_kernel, layers, members),
        in_specs=[VMEM] * 5,
        out_specs=VMEM,
        out_shape=out_shape,
        scratch_shapes=[pltpu.VMEM((count, held), BF16)],
        compiler_params=params(20),
        cost_estimate=SMALL,
    )(*tables, filter_taps, near, far)


def window(before, after, sign):
    (before_real, before_imag), (real, imag) = before, after
    if sign > 0:
        return before_real + imag, before_imag - real
    return before_real - imag, before_imag + real


def sum_products(pairs):
    real_sum = imag_sum = None
    for (tap_real, tap_imag), (real, imag) in pairs:
        real_part = tap_real * real - tap_imag * imag
        imag_part = tap_real * imag + tap_imag * real
        real_sum = real_part if real_sum is None else real_sum + real_part
        imag_sum = imag_part if imag_sum is None else imag_sum + imag_part
    return real_sum, imag_sum


def for_bins(rows, step, body):
    count = rows // (2 * step)
    for sign, first in ((1, 0), (-1, count)):

        @pl.loop(first, first + count)
        def _(index):
            body(pl.multiple_of(index * step, step), sign)


def reader(ref, rows, at, step):
    def read(*index):
        return ref[*index, pl.ds(at, step), :], ref[*index, pl.ds(at + rows, step), :]

    return read


def own_kernel(
    members, high_ref, low_ref, taps_ref, mine_ref, ahead_ref, across_ref, part_ref, first_ref, halo_ref, spectra
):
    member, _ = place(members)
    rows = high_ref.shape[1]
    for part in range(CHUNKS):
        blocks = [mine_ref[part, 0], mine_ref[part, 1], across_ref[part, 0], across_ref[part, 1]]
        for apart, block in enumerate(blocks):
            spectra[member ^ apart] = matmul(high_ref[...], block) + matmul(low_ref[...], block)
        first_ref[part] = spectra[0]
        for apart in range(2):
            block = ahead_ref[part, apart]
            halo_ref[part, member ^ apart] = matmul(high_ref[...], block) + matmul(low_ref[...], block)

        def body(at, sign):
            read = reader(spectra, rows, at, 8)
            taps_read = reader(taps_ref, rows, at, 8)
            taps = [taps_read(part, lag) for lag in range(members - 1)]
            blocks = [read(position) for position in range(members)]
            windows = [window(a, b, sign) for a, b in zip(blocks, blocks[1:])]
            for output in range(1, members):
                total = sum_products([(taps[lag], windows[output - 1 - lag]) for lag in range(output)])
                part_ref[part, output - 1, pl.ds(at, 8), :] = total[0]
                part_ref[part, output - 1, pl.ds(at + rows, 8), :] = total[1]

        for_bins(rows, 8, body)


def own_partials(tables, taps, *blocks):
    members = taps.shape[1]
    chunk = taps.shape[-1]
    rows = tables[0].shape[1]
    return pl.pallas_call(
        functools.partial(own_kernel, members),
        in_specs=[VMEM] * 6,
        out_specs=[VMEM] * 3,
        out_shape=[
            jax.ShapeDtypeStruct((CHUNKS, members - 1, 2 * rows, chunk), F32),
            jax.ShapeDtypeStruct((CHUNKS, 2 * rows, chunk), F32),
            jax.ShapeDtypeStruct((CHUNKS, members, 2 * rows, chunk), F32),
        ],
        scratch_shapes=[pltpu.VMEM((members, 2 * rows, chunk), F32)],
        compiler_params=params(20),
        cost_estimate=SMALL,
    )(*tables, taps, *blocks)


def mix_kernel(
    members,
    part,
    high_ref,
    low_ref,
    back_high_ref,
    back_low_ref,
    skip_ref,
    taps_ref,
    part_ref,
    first_ref,
    mine_ref,
    across_ref,
    beyond_ref,
    _,
    *refs,
):
    out_refs, (halo_ref, sums) = refs[:members], refs[members:]
    halo = halo_ref.at[part]

    def skip_of(part):
        chunk = out_refs[0].shape[1]
        if skip_ref.shape[1] == chunk:
            return skip_ref[pl.ds(part, 1), :]
        shares = skip_ref.shape[1] // (members * LANES) // CHUNKS
        picked = [
            skip_ref[:, aligned((part * shares + layer) * members + member, LANES)]
            for layer in range(shares)
        ]
        return jnp.concatenate(picked, axis=1)

    member, _ = place(members)
    rows = high_ref.shape[1]
    for apart in range(2, members):
        block = beyond_ref[apart - 2]
        halo[member ^ apart] = matmul(high_ref[...], block) + matmul(low_ref[...], block)

    def body(at, sign):
        read = reader(halo, rows, at, 8)
        taps_read = reader(taps_ref, rows, at, 8)
        taps = [taps_read(part, lag) for lag in range(members)]
        blocks = [read(position) for position in range(members)]
        blocks.append(reader(first_ref, rows, at, 8)(part))
        windows = [window(a, b, sign) for a, b in zip(blocks, blocks[1:])]
        for output in range(members):
            total = sum_products(
                [(taps[lag], windows[members - 1 + output - lag]) for lag in range(output, members)]
            )
            if output:
                before = reader(part_ref, rows, at, 8)(part, output - 1)
                total = total[0] + before[0], total[1] + before[1]
            sums[output, pl.ds(at, 8), :] = total[0]
            sums[output, pl.ds(at + rows, 8), :] = total[1]

    for_bins(rows, 8, body)
    blocks = [mine_ref[part, 0], mine_ref[part, 1], across_ref[part, 0], across_ref[part, 1]]
    skip = skip_of(part)
    for apart, block in enumerate(blocks):
        total = sums[member ^ apart]
        high = total.astype(BF16)
        low = (total - high.astype(F32)).astype(BF16)
        convolved = matmul(back_high_ref[...], high) + (
            matmul(back_high_ref[...], low) + matmul(back_low_ref[...], high)
        )
        mixed = convolved + skip * block.astype(F32)
        out_refs[apart][...] = mixed.astype(BF16)


def mixed_pieces(part, tables, back_tables, skip, taps, partial, first, mine, across, beyond, halo):
    members, chunk = taps.shape[1], taps.shape[-1]
    rows = tables[0].shape[1]
    operands = [*tables, *back_tables, skip, taps, partial, first, mine, across]
    *pieces, halo = pl.pallas_call(
        functools.partial(mix_kernel, members, part),
        in_specs=[VMEM] * (len(operands) + 2),
        out_specs=[VMEM] * (members + 1),
        out_shape=[jax.ShapeDtypeStruct((rows, chunk), BF16)] * members
        + [jax.ShapeDtypeStruct(halo.shape, F32)],
        input_output_aliases={len(operands) + 1: members},
        scratch_shapes=[pltpu.VMEM((members, 2 * rows, chunk), F32)],
        compiler_params=params(20),
        cost_estimate=SMALL,
    )(*operands, beyond, halo)
    return pieces, halo


def gate_kernel(layers, members, part, gate_ref, *refs):
    piece_refs, out_ref = refs[:members], refs[-1]
    member, _ = place(members)
    for apart in range(members):
        held = member ^ apart
        for layer in range(layers):
            lanes = aligned(layer * members + held, LANES)
            mixed = piece_refs[apart][:, layer * LANES : (layer + 1) * LANES].astype(F32)
            out_ref[:, lanes] = (gate_ref[:, lanes].astype(F32) * mixed).astype(BF16)


def gated_output(part, gate_out, pieces, layers, members, out):
    rows, channels = gate_out.shape
    chunk = channels // members // CHUNKS
    width = channels // (layers * members)
    wide = channels // CHUNKS
    if width != LANES:
        member, _ = place(members)
        stacked = jnp.stack(pieces)
        stacked = jnp.stack(
            [lax.dynamic_index_in_dim(stacked, member ^ d, 0, False) for d in range(members)]
        )
        mixed = stacked.reshape(members, rows, layers // CHUNKS, width).transpose(1, 2, 0, 3)
        gate = gate_out[:, part * wide : (part + 1) * wide].astype(F32)
        gated = (gate * mixed.reshape(rows, wide).astype(F32)).astype(BF16)
        return gated if out is None else jnp.concatenate([out, gated], axis=1)
    step = rows // 2
    there = pl.BlockSpec((step, wide), lambda r: (r, part))
    more = [] if out is None else [out]
    return pl.pallas_call(
        functools.partial(gate_kernel, layers // CHUNKS, members, part),
        grid=(2,),
        in_specs=[there]
        + [pl.BlockSpec((step, chunk), lambda r: (r, 0))] * members
        + [pl.BlockSpec(memory_space=pl.ANY)] * len(more),
        out_specs=there,
        out_shape=jax.ShapeDtypeStruct((rows, channels), BF16),
        input_output_aliases={members + 1: 0} if more else {},
        compiler_params=params(16),
        cost_estimate=SMALL,
    )(gate_out, *pieces, *more)


def on_device(gate_out, gate_in, values, filter_taps, skip_gain):
    rows, channels = values.shape
    length = lax.axis_size("ctx")
    members = filter_taps.shape[0] // rows
    layers = length // members
    width = channels // length
    member, _ = place(members)
    tables, back_tables = forward_tables(rows), inverse_tables(rows)

    def to_member(value, apart, ahead):
        pairs = [
            (i, (i // members + ahead) % layers * members + (i % members ^ apart))
            for i in range(length)
        ]
        return lax.ppermute(value, "ctx", pairs)

    def to_layer(value, apart):
        pairs = [(i, (i // members ^ apart) * members + i % members) for i in range(length)]
        return lax.ppermute(value, "ctx", pairs)

    half = near_half(filter_taps, layers, lax.axis_size("groups"))
    near = one_away = None
    if half is not None:
        two_away, one_away = to_layer(half, 2), to_layer(half, 1)
    same, other, *send = product_pieces(gate_in, values, one_away, layers, members)
    core = [to_member(piece, 1, 0) for piece in send]
    if half is not None:
        two_away, core = lax.optimization_barrier((two_away, core))
    mine, to_across, *to_beyond = payloads(same, other, core)
    if half is not None:
        three_away = to_layer(two_away, 1)
        near = joined([one_away, two_away, three_away])
    ahead = to_member(mine, 0, 1)
    beyond = [to_member(piece, 2, 1) for piece in to_beyond]
    across = to_member(to_across, 2, 0)
    taps = tap_spectra(tables, filter_taps, near, layers, members)
    partial, first, spectra = own_partials(tables, taps, mine, ahead, across)
    skip = skip_gain.reshape(1, channels)
    if width != LANES:
        skip = skip_gain.reshape(layers, members, width)
        skip = lax.dynamic_index_in_dim(skip, member, 1, False).reshape(CHUNKS, -1)
    out = None
    for part in range(CHUNKS):
        mixed, spectra = mixed_pieces(
            part, tables, back_tables, skip, taps, partial, first, mine, across, beyond[part], spectra
        )
        mixed = [mixed[0]] + [to_member(mixed[d], d, 0) for d in range(1, members)]
        out = gated_output(part, gate_out, mixed, layers, members, out)
    return out


def solution(mesh):
    in_specs = (
        P(("groups", "ctx"), None),
        P(("groups", "ctx"), None),
        P(("groups", "ctx"), None),
        P(None, "ctx"),
        P(),
    )
    out_specs = P(("groups", "ctx"), None)
    return jax.shard_map(
        on_device, mesh=mesh, in_specs=in_specs, out_specs=out_specs, check_vma=False
    )
```

```python
import functools

import jax
import jax.numpy as jnp
import ml_dtypes
import numpy as np
from jax import lax
from jax.experimental import pallas as pl
from jax.experimental.pallas import tpu as pltpu
from jax.sharding import PartitionSpec as P

LANES = 128
CHUNKS = 2
BF16 = jnp.bfloat16
F32 = jnp.float32
VMEM = pl.BlockSpec(memory_space=pltpu.VMEM)
SMALL = pl.CostEstimate(flops=1000, bytes_accessed=1000, transcendentals=0)


def two_parts(table):
    high = table.astype(ml_dtypes.bfloat16)
    low = (table - high.astype(np.float64)).astype(ml_dtypes.bfloat16)
    return jnp.asarray(high), jnp.asarray(low)


def bin_order(rows):
    return np.concatenate([np.arange(0, rows, 2), np.arange(1, rows, 2)])


def forward_tables(rows):
    bins = bin_order(rows)[:, None] + 0.5
    angle = bins * np.arange(rows)[None, :] * (np.pi / rows)
    return two_parts(np.concatenate([np.cos(angle), -np.sin(angle)], axis=0))


def inverse_tables(rows):
    bins = bin_order(rows)[None, :] + 0.5
    angle = bins * (np.arange(rows)[:, None] + rows) * (np.pi / rows)
    return two_parts(np.concatenate([np.cos(angle), -np.sin(angle)], axis=1) / rows)


def matmul(a, b):
    return jnp.dot(a, b, preferred_element_type=F32)


def params(mib):
    return pltpu.CompilerParams(vmem_limit_bytes=mib << 20)


def place(members):
    index = lax.axis_index("ctx")
    return lax.rem(index, members), lax.div(index, members)


def aligned(position, size):
    return pl.ds(pl.multiple_of(position * size, size), size)


def product_kernel(
    layers, members, gate_hbm, values_hbm, half_ref, keep_same_ref, keep_other_ref, *more
):
    del half_ref
    send_refs, (gate, values, sems) = more[:-3], more[-3:]
    member, _ = place(members)
    per_chunk = layers // CHUNKS
    count = sems.shape[1]
    step = gate.shape[0] // count

    def copies(index):
        rows = slice(index * step, (index + 1) * step)
        return [
            pltpu.make_async_copy(source.at[rows], target.at[rows], sems.at[which, index])
            for which, (source, target) in enumerate(((gate_hbm, gate), (values_hbm, values)))
        ]

    for index in range(count):
        for copy in copies(index):
            copy.start()
    refs = [
        lambda chunk, rows, lanes: keep_same_ref.at[chunk, rows, lanes],
        lambda chunk, rows, lanes: send_refs[2 * chunk].at[rows, lanes],
        lambda chunk, rows, lanes: keep_other_ref.at[chunk, rows, lanes],
        lambda chunk, rows, lanes: send_refs[2 * chunk + 1].at[rows, lanes],
    ]
    for index in range(count):
        rows = slice(index * step, (index + 1) * step)
        for copy in copies(index):
            copy.wait()
        for apart in range(members):
            held = member ^ apart
            for layer in range(layers):
                lanes = aligned(layer * members + held, LANES)
                gated = gate[rows, lanes].astype(F32) * values[rows, lanes].astype(F32)
                at = layer % per_chunk * LANES
                target = refs[apart](layer // per_chunk, rows, slice(at, at + LANES))
                target[...] = gated.astype(BF16)


def product_pieces(gate_in, values, half, layers, members):
    rows, channels = values.shape
    width = channels // (layers * members)
    chunk = channels // members // CHUNKS
    if width != LANES:
        member, _ = place(members)
        product = (gate_in.astype(F32) * values.astype(F32)).astype(BF16)
        product = product.reshape(rows, CHUNKS, layers // CHUNKS, members, width)
        product = product.transpose(3, 1, 0, 2, 4).reshape(members, CHUNKS, rows, chunk)
        pieces = [lax.dynamic_index_in_dim(product, member ^ d, 0, False) for d in range(members)]
        return pieces[0], pieces[2], pieces[1][0], pieces[3][0], pieces[1][1], pieces[3][1]
    count = 4
    there = pl.BlockSpec(memory_space=pltpu.HBM)
    return pl.pallas_call(
        functools.partial(product_kernel, layers, members),
        in_specs=[there, there, pl.BlockSpec(memory_space=pl.ANY)],
        out_specs=[VMEM] * (2 + 2 * CHUNKS),
        out_shape=[jax.ShapeDtypeStruct((CHUNKS, rows, chunk), BF16)] * 2
        + [jax.ShapeDtypeStruct((rows, chunk), BF16)] * (2 * CHUNKS),
        scratch_shapes=[pltpu.VMEM((rows, channels), BF16)] * 2 + [pltpu.SemaphoreType.DMA((2, count))],
        compiler_params=params(8),
        cost_estimate=SMALL,
    )(*(pltpu.with_memory_space_constraint(x, pltpu.HBM) for x in (gate_in, values)), half)


def pack_kernel(same_ref, other_ref, *refs):
    core_refs, (mine_ref, across_ref, *beyond_refs) = refs[: 2 * CHUNKS], refs[2 * CHUNKS :]
    for part in range(CHUNKS):
        mine_ref[part, 0] = same_ref[part]
        mine_ref[part, 1] = core_refs[2 * part][...]
        for target in (across_ref.at[part], beyond_refs[part]):
            target[0] = other_ref[part]
            target[1] = core_refs[2 * part + 1][...]


def payloads(same, other, core):
    _, rows, chunk = same.shape
    return pl.pallas_call(
        pack_kernel,
        in_specs=[VMEM] * (2 + len(core)),
        out_specs=[VMEM] * (2 + CHUNKS),
        out_shape=[jax.ShapeDtypeStruct((CHUNKS, 2, rows, chunk), BF16)] * 2
        + [jax.ShapeDtypeStruct((2, rows, chunk), BF16)] * CHUNKS,
        compiler_params=params(8),
        cost_estimate=SMALL,
    )(same, other, *core)


def join_kernel(*refs):
    at = 0
    for ref in refs[:-1]:
        count = ref.shape[0]
        refs[-1][at : at + count] = ref[...]
        at += count


def joined(pieces):
    return pl.pallas_call(
        join_kernel,
        in_specs=[VMEM] * len(pieces),
        out_specs=VMEM,
        out_shape=jax.ShapeDtypeStruct((sum(p.shape[0] for p in pieces), *pieces[0].shape[1:]), BF16),
        compiler_params=params(8),
        cost_estimate=SMALL,
    )(*pieces)


def put_tap_spectra(high_ref, low_ref, taps, out_ref):
    rows = high_ref.shape[1]
    chunk = out_ref.shape[-1]
    for part in range(CHUNKS):
        for lag in range(out_ref.shape[1]):
            block = taps[lag * rows : (lag + 1) * rows, part * chunk : (part + 1) * chunk]
            out_ref[part, lag] = matmul(high_ref[...], block) + matmul(low_ref[...], block)


def taps_kernel(layers, members, high_ref, low_ref, own_ref, near_ref, far_ref, out_ref, taps):
    _, layer = place(members)
    group = lax.axis_index("groups")
    half = near_ref.shape[1]
    near, far = aligned(group, half), aligned(1 - group, half)
    taps[:, aligned(layer, LANES)] = own_ref[...]
    for apart in range(1, layers):
        lanes = aligned(layer ^ apart, LANES)
        taps[near, lanes] = near_ref[apart - 1]
        taps[far, lanes] = far_ref[apart - 1]
    put_tap_spectra(high_ref, low_ref, taps, out_ref)


def near_half(filter_taps, layers, groups):
    count, width = filter_taps.shape
    if width != LANES or groups != 2 or layers != 4:
        return None
    start = lax.axis_index("groups") * (count // 2)
    return lax.dynamic_slice_in_dim(filter_taps, start, count // 2, 0)[None]


def tap_spectra(tables, filter_taps, near, layers, members):
    count, width = filter_taps.shape
    rows = tables[0].shape[1]
    held = width * layers
    out_shape = jax.ShapeDtypeStruct((CHUNKS, count // rows, 2 * rows, held // CHUNKS), F32)
    if near is None:
        ring = [[layer * members + member for layer in range(layers)] for member in range(members)]
        taps = lax.all_gather(filter_taps, "ctx", axis=1, tiled=True, axis_index_groups=ring)
        return pl.pallas_call(
            put_tap_spectra,
            in_specs=[VMEM] * 3,
            out_specs=VMEM,
            out_shape=out_shape,
            compiler_params=params(20),
            cost_estimate=SMALL,
        )(*tables, taps)
    far = lax.ppermute(near, "groups", [(0, 1), (1, 0)])
    return pl.pallas_call(
        functools.partial(taps_kernel, layers, members),
        in_specs=[VMEM] * 5,
        out_specs=VMEM,
        out_shape=out_shape,
        scratch_shapes=[pltpu.VMEM((count, held), BF16)],
        compiler_params=params(20),
        cost_estimate=SMALL,
    )(*tables, filter_taps, near, far)


def window(before, after, sign):
    (before_real, before_imag), (real, imag) = before, after
    if sign > 0:
        return before_real + imag, before_imag - real
    return before_real - imag, before_imag + real


def sum_products(pairs):
    real_sum = imag_sum = None
    for (tap_real, tap_imag), (real, imag) in pairs:
        real_part = tap_real * real - tap_imag * imag
        imag_part = tap_real * imag + tap_imag * real
        real_sum = real_part if real_sum is None else real_sum + real_part
        imag_sum = imag_part if imag_sum is None else imag_sum + imag_part
    return real_sum, imag_sum


def for_bins(rows, step, body):
    count = rows // (2 * step)
    for sign, first in ((1, 0), (-1, count)):

        @pl.loop(first, first + count)
        def _(index):
            body(pl.multiple_of(index * step, step), sign)


def reader(ref, rows, at, step):
    def read(*index):
        return ref[*index, pl.ds(at, step), :], ref[*index, pl.ds(at + rows, step), :]

    return read


def own_kernel(
    members, high_ref, low_ref, taps_ref, mine_ref, ahead_ref, across_ref, part_ref, first_ref, halo_ref, spectra
):
    member, _ = place(members)
    rows = high_ref.shape[1]
    for part in range(CHUNKS):
        blocks = [mine_ref[part, 0], mine_ref[part, 1], across_ref[part, 0], across_ref[part, 1]]
        for apart, block in enumerate(blocks):
            spectra[member ^ apart] = matmul(high_ref[...], block) + matmul(low_ref[...], block)
        first_ref[part] = spectra[0]
        for apart in range(2):
            block = ahead_ref[part, apart]
            halo_ref[part, member ^ apart] = matmul(high_ref[...], block) + matmul(low_ref[...], block)

        def body(at, sign):
            read = reader(spectra, rows, at, 8)
            taps_read = reader(taps_ref, rows, at, 8)
            taps = [taps_read(part, lag) for lag in range(members - 1)]
            blocks = [read(position) for position in range(members)]
            windows = [window(a, b, sign) for a, b in zip(blocks, blocks[1:])]
            for output in range(1, members):
                total = sum_products([(taps[lag], windows[output - 1 - lag]) for lag in range(output)])
                part_ref[part, output - 1, pl.ds(at, 8), :] = total[0]
                part_ref[part, output - 1, pl.ds(at + rows, 8), :] = total[1]

        for_bins(rows, 8, body)


def own_partials(tables, taps, *blocks):
    members = taps.shape[1]
    chunk = taps.shape[-1]
    rows = tables[0].shape[1]
    return pl.pallas_call(
        functools.partial(own_kernel, members),
        in_specs=[VMEM] * 6,
        out_specs=[VMEM] * 3,
        out_shape=[
            jax.ShapeDtypeStruct((CHUNKS, members - 1, 2 * rows, chunk), F32),
            jax.ShapeDtypeStruct((CHUNKS, 2 * rows, chunk), F32),
            jax.ShapeDtypeStruct((CHUNKS, members, 2 * rows, chunk), F32),
        ],
        scratch_shapes=[pltpu.VMEM((members, 2 * rows, chunk), F32)],
        compiler_params=params(20),
        cost_estimate=SMALL,
    )(*tables, taps, *blocks)


def mix_kernel(
    members,
    part,
    high_ref,
    low_ref,
    back_high_ref,
    back_low_ref,
    skip_ref,
    taps_ref,
    part_ref,
    first_ref,
    mine_ref,
    across_ref,
    beyond_ref,
    _,
    *refs,
):
    out_refs, (halo_ref, sums) = refs[:members], refs[members:]
    halo = halo_ref.at[part]

    def skip_of(part):
        chunk = out_refs[0].shape[1]
        if skip_ref.shape[1] == chunk:
            return skip_ref[pl.ds(part, 1), :]
        shares = skip_ref.shape[1] // (members * LANES) // CHUNKS
        picked = [
            skip_ref[:, aligned((part * shares + layer) * members + member, LANES)]
            for layer in range(shares)
        ]
        return jnp.concatenate(picked, axis=1)

    member, _ = place(members)
    rows = high_ref.shape[1]
    for apart in range(2, members):
        block = beyond_ref[apart - 2]
        halo[member ^ apart] = matmul(high_ref[...], block) + matmul(low_ref[...], block)

    def body(at, sign):
        read = reader(halo, rows, at, 8)
        taps_read = reader(taps_ref, rows, at, 8)
        taps = [taps_read(part, lag) for lag in range(members)]
        blocks = [read(position) for position in range(members)]
        blocks.append(reader(first_ref, rows, at, 8)(part))
        windows = [window(a, b, sign) for a, b in zip(blocks, blocks[1:])]
        for output in range(members):
            total = sum_products(
                [(taps[lag], windows[members - 1 + output - lag]) for lag in range(output, members)]
            )
            if output:
                before = reader(part_ref, rows, at, 8)(part, output - 1)
                total = total[0] + before[0], total[1] + before[1]
            sums[output, pl.ds(at, 8), :] = total[0]
            sums[output, pl.ds(at + rows, 8), :] = total[1]

    for_bins(rows, 8, body)
    blocks = [mine_ref[part, 0], mine_ref[part, 1], across_ref[part, 0], across_ref[part, 1]]
    skip = skip_of(part)
    for apart, block in enumerate(blocks):
        total = sums[member ^ apart]
        high = total.astype(BF16)
        low = (total - high.astype(F32)).astype(BF16)
        convolved = matmul(back_high_ref[...], high) + (
            matmul(back_high_ref[...], low) + matmul(back_low_ref[...], high)
        )
        mixed = convolved + skip * block.astype(F32)
        out_refs[apart][...] = mixed.astype(BF16)


def mixed_pieces(part, tables, back_tables, skip, taps, partial, first, mine, across, beyond, halo):
    members, chunk = taps.shape[1], taps.shape[-1]
    rows = tables[0].shape[1]
    operands = [*tables, *back_tables, skip, taps, partial, first, mine, across]
    *pieces, halo = pl.pallas_call(
        functools.partial(mix_kernel, members, part),
        in_specs=[VMEM] * (len(operands) + 2),
        out_specs=[VMEM] * (members + 1),
        out_shape=[jax.ShapeDtypeStruct((rows, chunk), BF16)] * members
        + [jax.ShapeDtypeStruct(halo.shape, F32)],
        input_output_aliases={len(operands) + 1: members},
        scratch_shapes=[pltpu.VMEM((members, 2 * rows, chunk), F32)],
        compiler_params=params(20),
        cost_estimate=SMALL,
    )(*operands, beyond, halo)
    return pieces, halo


def gate_kernel(layers, members, part, gate_ref, *refs):
    piece_refs, out_ref = refs[:members], refs[-1]
    member, _ = place(members)
    for apart in range(members):
        held = member ^ apart
        for layer in range(layers):
            lanes = aligned(layer * members + held, LANES)
            mixed = piece_refs[apart][:, layer * LANES : (layer + 1) * LANES].astype(F32)
            out_ref[:, lanes] = (gate_ref[:, lanes].astype(F32) * mixed).astype(BF16)


def gated_output(part, gate_out, pieces, layers, members, out):
    rows, channels = gate_out.shape
    chunk = channels // members // CHUNKS
    width = channels // (layers * members)
    wide = channels // CHUNKS
    if width != LANES:
        member, _ = place(members)
        stacked = jnp.stack(pieces)
        stacked = jnp.stack(
            [lax.dynamic_index_in_dim(stacked, member ^ d, 0, False) for d in range(members)]
        )
        mixed = stacked.reshape(members, rows, layers // CHUNKS, width).transpose(1, 2, 0, 3)
        gate = gate_out[:, part * wide : (part + 1) * wide].astype(F32)
        gated = (gate * mixed.reshape(rows, wide).astype(F32)).astype(BF16)
        return gated if out is None else jnp.concatenate([out, gated], axis=1)
    step = rows // 2
    there = pl.BlockSpec((step, wide), lambda r: (r, part))
    more = [] if out is None else [out]
    return pl.pallas_call(
        functools.partial(gate_kernel, layers // CHUNKS, members, part),
        grid=(2,),
        in_specs=[there]
        + [pl.BlockSpec((step, chunk), lambda r: (r, 0))] * members
        + [pl.BlockSpec(memory_space=pl.ANY)] * len(more),
        out_specs=there,
        out_shape=jax.ShapeDtypeStruct((rows, channels), BF16),
        input_output_aliases={members + 1: 0} if more else {},
        compiler_params=params(16),
        cost_estimate=SMALL,
    )(gate_out, *pieces, *more)


def on_device(gate_out, gate_in, values, filter_taps, skip_gain):
    rows, channels = values.shape
    length = lax.axis_size("ctx")
    members = filter_taps.shape[0] // rows
    layers = length // members
    width = channels // length
    member, _ = place(members)
    tables, back_tables = forward_tables(rows), inverse_tables(rows)

    def to_member(value, apart, ahead):
        pairs = [
            (i, (i // members + ahead) % layers * members + (i % members ^ apart))
            for i in range(length)
        ]
        return lax.ppermute(value, "ctx", pairs)

    def to_layer(value, apart):
        pairs = [(i, (i // members ^ apart) * members + i % members) for i in range(length)]
        return lax.ppermute(value, "ctx", pairs)

    half = near_half(filter_taps, layers, lax.axis_size("groups"))
    near = one_away = None
    if half is not None:
        two_away, one_away = to_layer(half, 2), to_layer(half, 1)
    same, other, *send = product_pieces(gate_in, values, half, layers, members)
    if half is not None:
        one_away, send = lax.optimization_barrier((one_away, send))
    core = [to_member(piece, 1, 0) for piece in send]
    if half is not None:
        two_away, core = lax.optimization_barrier((two_away, core))
    mine, to_across, *to_beyond = payloads(same, other, core)
    if half is not None:
        three_away = to_layer(two_away, 1)
        near = joined([one_away, two_away, three_away])
    ahead = to_member(mine, 0, 1)
    beyond = [to_member(piece, 2, 1) for piece in to_beyond]
    across = to_member(to_across, 2, 0)
    taps = tap_spectra(tables, filter_taps, near, layers, members)
    partial, first, spectra = own_partials(tables, taps, mine, ahead, across)
    skip = skip_gain.reshape(1, channels)
    if width != LANES:
        skip = skip_gain.reshape(layers, members, width)
        skip = lax.dynamic_index_in_dim(skip, member, 1, False).reshape(CHUNKS, -1)
    out = None
    for part in range(CHUNKS):
        mixed, spectra = mixed_pieces(
            part, tables, back_tables, skip, taps, partial, first, mine, across, beyond[part], spectra
        )
        mixed = [mixed[0]] + [to_member(mixed[d], d, 0) for d in range(1, members)]
        out = gated_output(part, gate_out, mixed, layers, members, out)
    return out


def solution(mesh):
    in_specs = (
        P(("groups", "ctx"), None),
        P(("groups", "ctx"), None),
        P(("groups", "ctx"), None),
        P(None, "ctx"),
        P(),
    )
    out_specs = P(("groups", "ctx"), None)
    return jax.shard_map(
        on_device, mesh=mesh, in_specs=in_specs, out_specs=out_specs, check_vma=False
    )
```

```python
import functools

import jax
import jax.numpy as jnp
import ml_dtypes
import numpy as np
from jax import lax
from jax.experimental import pallas as pl
from jax.experimental.pallas import tpu as pltpu
from jax.sharding import PartitionSpec as P

LANES = 128
CHUNKS = 2
BF16 = jnp.bfloat16
F32 = jnp.float32
VMEM = pl.BlockSpec(memory_space=pltpu.VMEM)
GATE_ORDER = (0, 2, 3, 1)
SMALL = pl.CostEstimate(flops=1000, bytes_accessed=1000, transcendentals=0)


def two_parts(table):
    high = table.astype(ml_dtypes.bfloat16)
    low = (table - high.astype(np.float64)).astype(ml_dtypes.bfloat16)
    return jnp.asarray(high), jnp.asarray(low)


def bin_order(rows):
    return np.concatenate([np.arange(0, rows, 2), np.arange(1, rows, 2)])


def forward_tables(rows):
    bins = bin_order(rows)[:, None] + 0.5
    angle = bins * np.arange(rows)[None, :] * (np.pi / rows)
    return two_parts(np.concatenate([np.cos(angle), -np.sin(angle)], axis=0))


def inverse_tables(rows):
    bins = bin_order(rows)[None, :] + 0.5
    angle = bins * (np.arange(rows)[:, None] + rows) * (np.pi / rows)
    return two_parts(np.concatenate([np.cos(angle), -np.sin(angle)], axis=1) / rows)


def matmul(a, b):
    return jnp.dot(a, b, preferred_element_type=F32)


def params(mib):
    return pltpu.CompilerParams(vmem_limit_bytes=mib << 20)


def place(members):
    index = lax.axis_index("ctx")
    return lax.rem(index, members), lax.div(index, members)


def aligned(position, size):
    return pl.ds(pl.multiple_of(position * size, size), size)


def product_kernel(
    layers, members, gate_hbm, values_hbm, half_ref, keep_same_ref, keep_other_ref, *more
):
    del half_ref
    send_refs, (gate, values, sems) = more[:-3], more[-3:]
    member, _ = place(members)
    per_chunk = layers // CHUNKS
    count = sems.shape[1]
    step = gate.shape[0] // count

    def copies(index):
        rows = slice(index * step, (index + 1) * step)
        return [
            pltpu.make_async_copy(source.at[rows], target.at[rows], sems.at[which, index])
            for which, (source, target) in enumerate(((gate_hbm, gate), (values_hbm, values)))
        ]

    for index in range(count):
        for copy in copies(index):
            copy.start()
    refs = [
        lambda chunk, rows, lanes: keep_same_ref.at[chunk, rows, lanes],
        lambda chunk, rows, lanes: send_refs[2 * chunk].at[rows, lanes],
        lambda chunk, rows, lanes: keep_other_ref.at[chunk, rows, lanes],
        lambda chunk, rows, lanes: send_refs[2 * chunk + 1].at[rows, lanes],
    ]
    for index in range(count):
        rows = slice(index * step, (index + 1) * step)
        for copy in copies(index):
            copy.wait()
        for apart in range(members):
            held = member ^ apart
            for layer in range(layers):
                lanes = aligned(layer * members + held, LANES)
                gated = gate[rows, lanes].astype(F32) * values[rows, lanes].astype(F32)
                at = layer % per_chunk * LANES
                target = refs[apart](layer // per_chunk, rows, slice(at, at + LANES))
                target[...] = gated.astype(BF16)


def product_pieces(gate_in, values, half, layers, members):
    rows, channels = values.shape
    width = channels // (layers * members)
    chunk = channels // members // CHUNKS
    if width != LANES:
        member, _ = place(members)
        product = (gate_in.astype(F32) * values.astype(F32)).astype(BF16)
        product = product.reshape(rows, CHUNKS, layers // CHUNKS, members, width)
        product = product.transpose(3, 1, 0, 2, 4).reshape(members, CHUNKS, rows, chunk)
        pieces = [lax.dynamic_index_in_dim(product, member ^ d, 0, False) for d in range(members)]
        return pieces[0], pieces[2], pieces[1][0], pieces[3][0], pieces[1][1], pieces[3][1]
    count = 4
    there = pl.BlockSpec(memory_space=pltpu.HBM)
    return pl.pallas_call(
        functools.partial(product_kernel, layers, members),
        in_specs=[there, there, pl.BlockSpec(memory_space=pl.ANY)],
        out_specs=[VMEM] * (2 + 2 * CHUNKS),
        out_shape=[jax.ShapeDtypeStruct((CHUNKS, rows, chunk), BF16)] * 2
        + [jax.ShapeDtypeStruct((rows, chunk), BF16)] * (2 * CHUNKS),
        scratch_shapes=[pltpu.VMEM((rows, channels), BF16)] * 2 + [pltpu.SemaphoreType.DMA((2, count))],
        compiler_params=params(8),
        cost_estimate=SMALL,
    )(*(pltpu.with_memory_space_constraint(x, pltpu.HBM) for x in (gate_in, values)), half)


def pack_kernel(same_ref, other_ref, *refs):
    core_refs, (mine_ref, across_ref, *beyond_refs) = refs[: 2 * CHUNKS], refs[2 * CHUNKS :]
    for part in range(CHUNKS):
        mine_ref[part, 0] = same_ref[part]
        mine_ref[part, 1] = core_refs[2 * part][...]
        for target in (across_ref.at[part], beyond_refs[part]):
            target[0] = other_ref[part]
            target[1] = core_refs[2 * part + 1][...]


def payloads(same, other, core):
    _, rows, chunk = same.shape
    return pl.pallas_call(
        pack_kernel,
        in_specs=[VMEM] * (2 + len(core)),
        out_specs=[VMEM] * (2 + CHUNKS),
        out_shape=[jax.ShapeDtypeStruct((CHUNKS, 2, rows, chunk), BF16)] * 2
        + [jax.ShapeDtypeStruct((2, rows, chunk), BF16)] * CHUNKS,
        compiler_params=params(8),
        cost_estimate=SMALL,
    )(same, other, *core)


def join_kernel(*refs):
    at = 0
    for ref in refs[:-1]:
        count = ref.shape[0]
        refs[-1][at : at + count] = ref[...]
        at += count


def joined(pieces):
    return pl.pallas_call(
        join_kernel,
        in_specs=[VMEM] * len(pieces),
        out_specs=VMEM,
        out_shape=jax.ShapeDtypeStruct((sum(p.shape[0] for p in pieces), *pieces[0].shape[1:]), BF16),
        compiler_params=params(8),
        cost_estimate=SMALL,
    )(*pieces)


def put_tap_spectra(high_ref, low_ref, taps, out_ref):
    rows = high_ref.shape[1]
    chunk = out_ref.shape[-1]
    for part in range(CHUNKS):
        for lag in range(out_ref.shape[1]):
            block = taps[lag * rows : (lag + 1) * rows, part * chunk : (part + 1) * chunk]
            out_ref[part, lag] = matmul(high_ref[...], block) + matmul(low_ref[...], block)


def taps_kernel(layers, members, high_ref, low_ref, own_ref, near_ref, far_ref, out_ref, taps):
    _, layer = place(members)
    group = lax.axis_index("groups")
    half = near_ref.shape[1]
    near, far = aligned(group, half), aligned(1 - group, half)
    taps[:, aligned(layer, LANES)] = own_ref[...]
    for apart in range(1, layers):
        lanes = aligned(layer ^ apart, LANES)
        taps[near, lanes] = near_ref[apart - 1]
        taps[far, lanes] = far_ref[apart - 1]
    put_tap_spectra(high_ref, low_ref, taps, out_ref)


def half_kernel(taps_hbm, half_ref, sem):
    half = half_ref.shape[1]
    rows = aligned(lax.axis_index("groups"), half)
    copy = pltpu.make_async_copy(taps_hbm.at[rows], half_ref.at[0], sem)
    copy.start()
    copy.wait()


def near_half(filter_taps, layers, groups):
    count, width = filter_taps.shape
    if width != LANES or groups != 2 or layers != 4:
        return None
    return pl.pallas_call(
        half_kernel,
        in_specs=[pl.BlockSpec(memory_space=pltpu.HBM)],
        out_specs=VMEM,
        out_shape=jax.ShapeDtypeStruct((1, count // 2, width), BF16),
        scratch_shapes=[pltpu.SemaphoreType.DMA],
        compiler_params=params(8),
        cost_estimate=SMALL,
    )(pltpu.with_memory_space_constraint(filter_taps, pltpu.HBM))


def tap_spectra(tables, filter_taps, near, layers, members):
    count, width = filter_taps.shape
    rows = tables[0].shape[1]
    held = width * layers
    out_shape = jax.ShapeDtypeStruct((CHUNKS, count // rows, 2 * rows, held // CHUNKS), F32)
    if near is None:
        ring = [[layer * members + member for layer in range(layers)] for member in range(members)]
        taps = lax.all_gather(filter_taps, "ctx", axis=1, tiled=True, axis_index_groups=ring)
        return pl.pallas_call(
            put_tap_spectra,
            in_specs=[VMEM] * 3,
            out_specs=VMEM,
            out_shape=out_shape,
            compiler_params=params(20),
            cost_estimate=SMALL,
        )(*tables, taps)
    far = lax.ppermute(near, "groups", [(0, 1), (1, 0)])
    return pl.pallas_call(
        functools.partial(taps_kernel, layers, members),
        in_specs=[VMEM] * 5,
        out_specs=VMEM,
        out_shape=out_shape,
        scratch_shapes=[pltpu.VMEM((count, held), BF16)],
        compiler_params=params(20),
        cost_estimate=SMALL,
    )(*tables, filter_taps, near, far)


def window(before, after, sign):
    (before_real, before_imag), (real, imag) = before, after
    if sign > 0:
        return before_real + imag, before_imag - real
    return before_real - imag, before_imag + real


def sum_products(pairs):
    real_sum = imag_sum = None
    for (tap_real, tap_imag), (real, imag) in pairs:
        real_part = tap_real * real - tap_imag * imag
        imag_part = tap_real * imag + tap_imag * real
        real_sum = real_part if real_sum is None else real_sum + real_part
        imag_sum = imag_part if imag_sum is None else imag_sum + imag_part
    return real_sum, imag_sum


def for_bins(rows, step, body):
    count = rows // (2 * step)
    for sign, first in ((1, 0), (-1, count)):

        @pl.loop(first, first + count)
        def _(index):
            body(pl.multiple_of(index * step, step), sign)


def reader(ref, rows, at, step):
    def read(*index):
        return ref[*index, pl.ds(at, step), :], ref[*index, pl.ds(at + rows, step), :]

    return read


def own_kernel(
    members, high_ref, low_ref, taps_ref, mine_ref, ahead_ref, across_ref, part_ref, first_ref, halo_ref, spectra
):
    member, _ = place(members)
    rows = high_ref.shape[1]
    for part in range(CHUNKS):
        blocks = [mine_ref[part, 0], mine_ref[part, 1], across_ref[part, 0], across_ref[part, 1]]
        for apart, block in enumerate(blocks):
            spectra[member ^ apart] = matmul(high_ref[...], block) + matmul(low_ref[...], block)
        first_ref[part] = spectra[0]
        for apart in range(2):
            block = ahead_ref[part, apart]
            halo_ref[part, member ^ apart] = matmul(high_ref[...], block) + matmul(low_ref[...], block)

        def body(at, sign):
            read = reader(spectra, rows, at, 8)
            taps_read = reader(taps_ref, rows, at, 8)
            taps = [taps_read(part, lag) for lag in range(members - 1)]
            blocks = [read(position) for position in range(members)]
            windows = [window(a, b, sign) for a, b in zip(blocks, blocks[1:])]
            for output in range(1, members):
                total = sum_products([(taps[lag], windows[output - 1 - lag]) for lag in range(output)])
                part_ref[part, output - 1, pl.ds(at, 8), :] = total[0]
                part_ref[part, output - 1, pl.ds(at + rows, 8), :] = total[1]

        for_bins(rows, 8, body)


def own_partials(tables, taps, *blocks):
    members = taps.shape[1]
    chunk = taps.shape[-1]
    rows = tables[0].shape[1]
    return pl.pallas_call(
        functools.partial(own_kernel, members),
        in_specs=[VMEM] * 6,
        out_specs=[VMEM] * 3,
        out_shape=[
            jax.ShapeDtypeStruct((CHUNKS, members - 1, 2 * rows, chunk), F32),
            jax.ShapeDtypeStruct((CHUNKS, 2 * rows, chunk), F32),
            jax.ShapeDtypeStruct((CHUNKS, members, 2 * rows, chunk), F32),
        ],
        scratch_shapes=[pltpu.VMEM((members, 2 * rows, chunk), F32)],
        compiler_params=params(20),
        cost_estimate=SMALL,
    )(*tables, taps, *blocks)


def mix_kernel(
    members,
    part,
    high_ref,
    low_ref,
    back_high_ref,
    back_low_ref,
    skip_ref,
    taps_ref,
    part_ref,
    first_ref,
    mine_ref,
    across_ref,
    beyond_ref,
    _,
    *refs,
):
    out_refs, (halo_ref, sums) = refs[:members], refs[members:]
    halo = halo_ref.at[part]

    def skip_of(part):
        chunk = out_refs[0].shape[1]
        if skip_ref.shape[1] == chunk:
            return skip_ref[pl.ds(part, 1), :]
        shares = skip_ref.shape[1] // (members * LANES) // CHUNKS
        picked = [
            skip_ref[:, aligned((part * shares + layer) * members + member, LANES)]
            for layer in range(shares)
        ]
        return jnp.concatenate(picked, axis=1)

    member, _ = place(members)
    rows = high_ref.shape[1]
    for apart in range(2, members):
        block = beyond_ref[apart - 2]
        halo[member ^ apart] = matmul(high_ref[...], block) + matmul(low_ref[...], block)

    def body(at, sign):
        read = reader(halo, rows, at, 8)
        taps_read = reader(taps_ref, rows, at, 8)
        taps = [taps_read(part, lag) for lag in range(members)]
        blocks = [read(position) for position in range(members)]
        blocks.append(reader(first_ref, rows, at, 8)(part))
        windows = [window(a, b, sign) for a, b in zip(blocks, blocks[1:])]
        for output in range(members):
            total = sum_products(
                [(taps[lag], windows[members - 1 + output - lag]) for lag in range(output, members)]
            )
            if output:
                before = reader(part_ref, rows, at, 8)(part, output - 1)
                total = total[0] + before[0], total[1] + before[1]
            sums[output, pl.ds(at, 8), :] = total[0]
            sums[output, pl.ds(at + rows, 8), :] = total[1]

    for_bins(rows, 8, body)
    blocks = [mine_ref[part, 0], mine_ref[part, 1], across_ref[part, 0], across_ref[part, 1]]
    skip = skip_of(part)
    for apart, block in enumerate(blocks):
        total = sums[member ^ apart]
        high = total.astype(BF16)
        low = (total - high.astype(F32)).astype(BF16)
        convolved = matmul(back_high_ref[...], high) + (
            matmul(back_high_ref[...], low) + matmul(back_low_ref[...], high)
        )
        mixed = convolved + skip * block.astype(F32)
        out_refs[apart][...] = mixed.astype(BF16)


def mixed_pieces(part, tables, back_tables, skip, taps, partial, first, mine, across, beyond, halo):
    members, chunk = taps.shape[1], taps.shape[-1]
    rows = tables[0].shape[1]
    operands = [*tables, *back_tables, skip, taps, partial, first, mine, across]
    *pieces, halo = pl.pallas_call(
        functools.partial(mix_kernel, members, part),
        in_specs=[VMEM] * (len(operands) + 2),
        out_specs=[VMEM] * (members + 1),
        out_shape=[jax.ShapeDtypeStruct((rows, chunk), BF16)] * members
        + [jax.ShapeDtypeStruct(halo.shape, F32)],
        input_output_aliases={len(operands) + 1: members},
        scratch_shapes=[pltpu.VMEM((members, 2 * rows, chunk), F32)],
        compiler_params=params(20),
        cost_estimate=SMALL,
    )(*operands, beyond, halo)
    return pieces, halo


def gate_kernel(layers, members, part, gate_ref, *refs):
    piece_refs, (out_hbm, out, sems) = refs[:members], refs[-3:]
    member, _ = place(members)
    count = sems.shape[0]
    step, wide = out.shape[0] // count, out.shape[1]
    here = slice(part * wide, (part + 1) * wide)
    copies = []
    for index in range(count):
        rows = slice(index * step, (index + 1) * step)
        for which, apart in enumerate(GATE_ORDER):
            held = member ^ apart
            for layer in range(layers):
                lanes = aligned(layer * members + held, LANES)
                source = aligned((part * layers + layer) * members + held, LANES)
                mixed = piece_refs[which][rows, layer * LANES : (layer + 1) * LANES].astype(F32)
                out[rows, lanes] = (gate_ref[rows, source].astype(F32) * mixed).astype(BF16)
        copies.append(pltpu.make_async_copy(out.at[rows], out_hbm.at[rows, here], sems.at[index]))
        copies[-1].start()
    for copy in copies:
        copy.wait()


def gated_output(part, gate_out, pieces, layers, members, out):
    rows, channels = gate_out.shape
    chunk = channels // members // CHUNKS
    width = channels // (layers * members)
    wide = channels // CHUNKS
    if width != LANES:
        member, _ = place(members)
        stacked = jnp.stack(pieces)
        stacked = jnp.stack(
            [lax.dynamic_index_in_dim(stacked, member ^ d, 0, False) for d in range(members)]
        )
        mixed = stacked.reshape(members, rows, layers // CHUNKS, width).transpose(1, 2, 0, 3)
        gate = gate_out[:, part * wide : (part + 1) * wide].astype(F32)
        gated = (gate * mixed.reshape(rows, wide).astype(F32)).astype(BF16)
        return gated if out is None else jnp.concatenate([out, gated], axis=1)
    more = [] if out is None else [out]
    count = 2
    return pl.pallas_call(
        functools.partial(gate_kernel, layers // CHUNKS, members, part),
        in_specs=[VMEM] * (1 + members) + [pl.BlockSpec(memory_space=pl.ANY)] * len(more),
        out_specs=pl.BlockSpec(memory_space=pl.ANY),
        out_shape=jax.ShapeDtypeStruct((rows, channels), BF16),
        scratch_shapes=[pltpu.VMEM((rows, wide), BF16), pltpu.SemaphoreType.DMA((count,))],
        input_output_aliases={members + 1: 0} if more else {},
        compiler_params=params(8),
        cost_estimate=SMALL,
    )(gate_out, *(pieces[apart] for apart in GATE_ORDER), *more)


def on_device(gate_out, gate_in, values, filter_taps, skip_gain):
    rows, channels = values.shape
    length = lax.axis_size("ctx")
    members = filter_taps.shape[0] // rows
    layers = length // members
    width = channels // length
    member, _ = place(members)
    tables, back_tables = forward_tables(rows), inverse_tables(rows)

    def to_member(value, apart, ahead):
        pairs = [
            (i, (i // members + ahead) % layers * members + (i % members ^ apart))
            for i in range(length)
        ]
        return lax.ppermute(value, "ctx", pairs)

    def to_layer(value, apart):
        pairs = [(i, (i // members ^ apart) * members + i % members) for i in range(length)]
        return lax.ppermute(value, "ctx", pairs)

    half = near_half(filter_taps, layers, lax.axis_size("groups"))
    near = one_away = None
    if half is not None:
        two_away, one_away = to_layer(half, 2), to_layer(half, 1)
    same, other, *send = product_pieces(gate_in, values, half, layers, members)
    if half is not None:
        one_away, send = lax.optimization_barrier((one_away, send))
    core = [to_member(piece, 1, 0) for piece in send]
    if half is not None:
        two_away, core = lax.optimization_barrier((two_away, core))
    mine, to_across, *to_beyond = payloads(same, other, core)
    if half is not None:
        three_away = to_layer(two_away, 1)
        near = joined([one_away, two_away, three_away])
    ahead = to_member(mine, 0, 1)
    beyond = [to_member(piece, 2, 1) for piece in to_beyond]
    across = to_member(to_across, 2, 0)
    taps = tap_spectra(tables, filter_taps, near, layers, members)
    partial, first, spectra = own_partials(tables, taps, mine, ahead, across)
    skip = skip_gain.reshape(1, channels)
    if width != LANES:
        skip = skip_gain.reshape(layers, members, width)
        skip = lax.dynamic_index_in_dim(skip, member, 1, False).reshape(CHUNKS, -1)
    out = None
    for part in range(CHUNKS):
        mixed, spectra = mixed_pieces(
            part, tables, back_tables, skip, taps, partial, first, mine, across, beyond[part], spectra
        )
        mixed = [mixed[0]] + [to_member(mixed[d], d, 0) for d in range(1, members)]
        out = gated_output(part, gate_out, mixed, layers, members, out)
    return out


def solution(mesh):
    in_specs = (
        P(("groups", "ctx"), None),
        P(("groups", "ctx"), None),
        P(("groups", "ctx"), None),
        P(None, "ctx"),
        P(),
    )
    out_specs = P(("groups", "ctx"), None)
    return jax.shard_map(
        on_device, mesh=mesh, in_specs=in_specs, out_specs=out_specs, check_vma=False
    )
```

```python
import functools

import jax
import jax.numpy as jnp
import ml_dtypes
import numpy as np
from jax import lax
from jax.experimental import pallas as pl
from jax.experimental.pallas import tpu as pltpu
from jax.sharding import PartitionSpec as P

LANES = 128
CHUNKS = 2
BF16 = jnp.bfloat16
F32 = jnp.float32
VMEM = pl.BlockSpec(memory_space=pltpu.VMEM)
GATE_ORDER = (0, 2, 3, 1)
SMALL = pl.CostEstimate(flops=1000, bytes_accessed=1000, transcendentals=0)


def two_parts(table):
    high = table.astype(ml_dtypes.bfloat16)
    low = (table - high.astype(np.float64)).astype(ml_dtypes.bfloat16)
    return jnp.asarray(high), jnp.asarray(low)


def bin_order(rows):
    return np.concatenate([np.arange(0, rows, 2), np.arange(1, rows, 2)])


def forward_tables(rows):
    bins = bin_order(rows)[:, None] + 0.5
    angle = bins * np.arange(rows)[None, :] * (np.pi / rows)
    return two_parts(np.concatenate([np.cos(angle), -np.sin(angle)], axis=0))


def inverse_tables(rows):
    bins = bin_order(rows)[None, :] + 0.5
    angle = bins * (np.arange(rows)[:, None] + rows) * (np.pi / rows)
    return two_parts(np.concatenate([np.cos(angle), -np.sin(angle)], axis=1) / rows)


def matmul(a, b):
    return jnp.dot(a, b, preferred_element_type=F32)


def params(mib):
    return pltpu.CompilerParams(vmem_limit_bytes=mib << 20)


def place(members):
    index = lax.axis_index("ctx")
    return lax.rem(index, members), lax.div(index, members)


def aligned(position, size):
    return pl.ds(pl.multiple_of(position * size, size), size)


def product_kernel(
    layers, members, gate_hbm, values_hbm, half_ref, keep_same_ref, keep_other_ref, *more
):
    del half_ref
    send_refs, (gate, values, sems) = more[:-3], more[-3:]
    member, _ = place(members)
    per_chunk = layers // CHUNKS
    count = sems.shape[1]
    step = gate.shape[0] // count

    def copies(index):
        rows = slice(index * step, (index + 1) * step)
        return [
            pltpu.make_async_copy(source.at[rows], target.at[rows], sems.at[which, index])
            for which, (source, target) in enumerate(((gate_hbm, gate), (values_hbm, values)))
        ]

    for index in range(count):
        for copy in copies(index):
            copy.start()
    refs = [
        lambda chunk, rows, lanes: keep_same_ref.at[chunk, rows, lanes],
        lambda chunk, rows, lanes: send_refs[2 * chunk].at[rows, lanes],
        lambda chunk, rows, lanes: keep_other_ref.at[chunk, rows, lanes],
        lambda chunk, rows, lanes: send_refs[2 * chunk + 1].at[rows, lanes],
    ]
    for index in range(count):
        rows = slice(index * step, (index + 1) * step)
        for copy in copies(index):
            copy.wait()
        for apart in range(members):
            held = member ^ apart
            for layer in range(layers):
                lanes = aligned(layer * members + held, LANES)
                gated = gate[rows, lanes].astype(F32) * values[rows, lanes].astype(F32)
                at = layer % per_chunk * LANES
                target = refs[apart](layer // per_chunk, rows, slice(at, at + LANES))
                target[...] = gated.astype(BF16)


def product_pieces(gate_in, values, half, layers, members):
    rows, channels = values.shape
    width = channels // (layers * members)
    chunk = channels // members // CHUNKS
    if width != LANES:
        member, _ = place(members)
        product = (gate_in.astype(F32) * values.astype(F32)).astype(BF16)
        product = product.reshape(rows, CHUNKS, layers // CHUNKS, members, width)
        product = product.transpose(3, 1, 0, 2, 4).reshape(members, CHUNKS, rows, chunk)
        pieces = [lax.dynamic_index_in_dim(product, member ^ d, 0, False) for d in range(members)]
        return pieces[0], pieces[2], pieces[1][0], pieces[3][0], pieces[1][1], pieces[3][1]
    count = 4
    there = pl.BlockSpec(memory_space=pltpu.HBM)
    return pl.pallas_call(
        functools.partial(product_kernel, layers, members),
        in_specs=[there, there, pl.BlockSpec(memory_space=pl.ANY)],
        out_specs=[VMEM] * (2 + 2 * CHUNKS),
        out_shape=[jax.ShapeDtypeStruct((CHUNKS, rows, chunk), BF16)] * 2
        + [jax.ShapeDtypeStruct((rows, chunk), BF16)] * (2 * CHUNKS),
        scratch_shapes=[pltpu.VMEM((rows, channels), BF16)] * 2 + [pltpu.SemaphoreType.DMA((2, count))],
        compiler_params=params(8),
        cost_estimate=SMALL,
    )(*(pltpu.with_memory_space_constraint(x, pltpu.HBM) for x in (gate_in, values)), half)


def pack_kernel(same_ref, other_ref, *refs):
    core_refs, (mine_ref, across_ref, *beyond_refs) = refs[: 2 * CHUNKS], refs[2 * CHUNKS :]
    for part in range(CHUNKS):
        mine_ref[part, 0] = same_ref[part]
        mine_ref[part, 1] = core_refs[2 * part][...]
        for target in (across_ref.at[part], beyond_refs[part]):
            target[0] = other_ref[part]
            target[1] = core_refs[2 * part + 1][...]


def payloads(same, other, core):
    _, rows, chunk = same.shape
    return pl.pallas_call(
        pack_kernel,
        in_specs=[VMEM] * (2 + len(core)),
        out_specs=[VMEM] * (2 + CHUNKS),
        out_shape=[jax.ShapeDtypeStruct((CHUNKS, 2, rows, chunk), BF16)] * 2
        + [jax.ShapeDtypeStruct((2, rows, chunk), BF16)] * CHUNKS,
        compiler_params=params(8),
        cost_estimate=SMALL,
    )(same, other, *core)


def join_kernel(*refs):
    at = 0
    for ref in refs[:-1]:
        count = ref.shape[0]
        refs[-1][at : at + count] = ref[...]
        at += count


def joined(pieces):
    return pl.pallas_call(
        join_kernel,
        in_specs=[VMEM] * len(pieces),
        out_specs=VMEM,
        out_shape=jax.ShapeDtypeStruct((sum(p.shape[0] for p in pieces), *pieces[0].shape[1:]), BF16),
        compiler_params=params(8),
        cost_estimate=SMALL,
    )(*pieces)


def put_tap_spectra(high_ref, low_ref, taps, out_ref):
    rows = high_ref.shape[1]
    chunk = out_ref.shape[-1]
    for part in range(CHUNKS):
        for lag in range(out_ref.shape[1]):
            block = taps[lag * rows : (lag + 1) * rows, part * chunk : (part + 1) * chunk]
            out_ref[part, lag] = matmul(high_ref[...], block) + matmul(low_ref[...], block)


def taps_kernel(layers, members, high_ref, low_ref, own_ref, near_ref, far_ref, out_ref, taps):
    _, layer = place(members)
    group = lax.axis_index("groups")
    half = near_ref.shape[1]
    near, far = aligned(group, half), aligned(1 - group, half)
    taps[:, aligned(layer, LANES)] = own_ref[...]
    for apart in range(1, layers):
        lanes = aligned(layer ^ apart, LANES)
        taps[near, lanes] = near_ref[apart - 1]
        taps[far, lanes] = far_ref[apart - 1]
    put_tap_spectra(high_ref, low_ref, taps, out_ref)


def half_kernel(taps_hbm, half_ref, sem):
    half = half_ref.shape[1]
    rows = aligned(lax.axis_index("groups"), half)
    copy = pltpu.make_async_copy(taps_hbm.at[rows], half_ref.at[0], sem)
    copy.start()
    copy.wait()


def near_half(filter_taps, layers, groups):
    count, width = filter_taps.shape
    if width != LANES or groups != 2 or layers != 4:
        return None
    return pl.pallas_call(
        half_kernel,
        in_specs=[pl.BlockSpec(memory_space=pltpu.HBM)],
        out_specs=VMEM,
        out_shape=jax.ShapeDtypeStruct((1, count // 2, width), BF16),
        scratch_shapes=[pltpu.SemaphoreType.DMA],
        compiler_params=params(8),
        cost_estimate=SMALL,
    )(pltpu.with_memory_space_constraint(filter_taps, pltpu.HBM))


def tap_spectra(tables, filter_taps, near, layers, members):
    count, width = filter_taps.shape
    rows = tables[0].shape[1]
    held = width * layers
    out_shape = jax.ShapeDtypeStruct((CHUNKS, count // rows, 2 * rows, held // CHUNKS), F32)
    if near is None:
        ring = [[layer * members + member for layer in range(layers)] for member in range(members)]
        taps = lax.all_gather(filter_taps, "ctx", axis=1, tiled=True, axis_index_groups=ring)
        return pl.pallas_call(
            put_tap_spectra,
            in_specs=[VMEM] * 3,
            out_specs=VMEM,
            out_shape=out_shape,
            compiler_params=params(20),
            cost_estimate=SMALL,
        )(*tables, taps)
    far = lax.ppermute(near, "groups", [(0, 1), (1, 0)])
    return pl.pallas_call(
        functools.partial(taps_kernel, layers, members),
        in_specs=[VMEM] * 5,
        out_specs=VMEM,
        out_shape=out_shape,
        scratch_shapes=[pltpu.VMEM((count, held), BF16)],
        compiler_params=params(20),
        cost_estimate=SMALL,
    )(*tables, filter_taps, near, far)


def window(before, after, sign):
    (before_real, before_imag), (real, imag) = before, after
    if sign > 0:
        return before_real + imag, before_imag - real
    return before_real - imag, before_imag + real


def sum_products(pairs):
    real_sum = imag_sum = None
    for (tap_real, tap_imag), (real, imag) in pairs:
        real_part = tap_real * real - tap_imag * imag
        imag_part = tap_real * imag + tap_imag * real
        real_sum = real_part if real_sum is None else real_sum + real_part
        imag_sum = imag_part if imag_sum is None else imag_sum + imag_part
    return real_sum, imag_sum


def for_bins(rows, step, body):
    count = rows // (2 * step)
    for sign, first in ((1, 0), (-1, count)):

        @pl.loop(first, first + count)
        def _(index):
            body(pl.multiple_of(index * step, step), sign)


def reader(ref, rows, at, step):
    def read(*index):
        return ref[*index, pl.ds(at, step), :], ref[*index, pl.ds(at + rows, step), :]

    return read


def own_kernel(
    members, high_ref, low_ref, taps_ref, mine_ref, ahead_ref, across_ref, part_ref, first_ref, halo_ref, spectra
):
    member, _ = place(members)
    rows = high_ref.shape[1]
    for part in range(CHUNKS):
        blocks = [mine_ref[part, 0], mine_ref[part, 1], across_ref[part, 0], across_ref[part, 1]]
        for apart, block in enumerate(blocks):
            spectra[member ^ apart] = matmul(high_ref[...], block) + matmul(low_ref[...], block)
        first_ref[part] = spectra[0]
        for apart in range(2):
            block = ahead_ref[part, apart]
            halo_ref[part, (member ^ apart) % 2] = matmul(high_ref[...], block) + matmul(low_ref[...], block)

        def body(at, sign):
            read = reader(spectra, rows, at, 8)
            taps_read = reader(taps_ref, rows, at, 8)
            taps = [taps_read(part, lag) for lag in range(members - 1)]
            blocks = [read(position) for position in range(members)]
            windows = [window(a, b, sign) for a, b in zip(blocks, blocks[1:])]
            for output in range(1, members):
                total = sum_products([(taps[lag], windows[output - 1 - lag]) for lag in range(output)])
                part_ref[part, output - 1, pl.ds(at, 8), :] = total[0]
                part_ref[part, output - 1, pl.ds(at + rows, 8), :] = total[1]

        for_bins(rows, 8, body)


def own_partials(tables, taps, *blocks):
    members = taps.shape[1]
    chunk = taps.shape[-1]
    rows = tables[0].shape[1]
    return pl.pallas_call(
        functools.partial(own_kernel, members),
        in_specs=[VMEM] * 6,
        out_specs=[VMEM] * 3,
        out_shape=[
            jax.ShapeDtypeStruct((CHUNKS, members - 1, 2 * rows, chunk), F32),
            jax.ShapeDtypeStruct((CHUNKS, 2 * rows, chunk), F32),
            jax.ShapeDtypeStruct((CHUNKS, members // 2, 2 * rows, chunk), F32),
        ],
        scratch_shapes=[pltpu.VMEM((members, 2 * rows, chunk), F32)],
        compiler_params=params(20),
        cost_estimate=SMALL,
    )(*tables, taps, *blocks)


def mix_kernel(
    members,
    part,
    high_ref,
    low_ref,
    back_high_ref,
    back_low_ref,
    skip_ref,
    taps_ref,
    part_ref,
    first_ref,
    mine_ref,
    across_ref,
    beyond_ref,
    ahead_ref,
    _,
    *refs,
):
    out_refs, (beyond, sums) = refs[:members], refs[members:]

    def skip_of(part):
        chunk = out_refs[0].shape[1]
        if skip_ref.shape[1] == chunk:
            return skip_ref[pl.ds(part, 1), :]
        shares = skip_ref.shape[1] // (members * LANES) // CHUNKS
        picked = [
            skip_ref[:, aligned((part * shares + layer) * members + member, LANES)]
            for layer in range(shares)
        ]
        return jnp.concatenate(picked, axis=1)

    member, _ = place(members)
    rows = high_ref.shape[1]
    for apart in range(2, members):
        block = beyond_ref[apart - 2]
        beyond[(member ^ apart) % 2] = matmul(high_ref[...], block) + matmul(low_ref[...], block)

    def body(pair, at, sign):
        halves = [reader(beyond, rows, at, 8)] * (members // 2)
        halves[pair] = functools.partial(reader(ahead_ref, rows, at, 8), part)
        taps_read = reader(taps_ref, rows, at, 8)
        taps = [taps_read(part, lag) for lag in range(members)]
        blocks = [halves[position // 2](position % 2) for position in range(members)]
        blocks.append(reader(first_ref, rows, at, 8)(part))
        windows = [window(a, b, sign) for a, b in zip(blocks, blocks[1:])]
        for output in range(members):
            total = sum_products(
                [(taps[lag], windows[members - 1 + output - lag]) for lag in range(output, members)]
            )
            if output:
                before = reader(part_ref, rows, at, 8)(part, output - 1)
                total = total[0] + before[0], total[1] + before[1]
            sums[output, pl.ds(at, 8), :] = total[0]
            sums[output, pl.ds(at + rows, 8), :] = total[1]

    for pair in range(members // 2):
        pl.when(member // 2 == pair)(
            functools.partial(for_bins, rows, 8, functools.partial(body, pair))
        )
    blocks = [mine_ref[part, 0], mine_ref[part, 1], across_ref[part, 0], across_ref[part, 1]]
    skip = skip_of(part)
    for apart, block in enumerate(blocks):
        total = sums[member ^ apart]
        high = total.astype(BF16)
        low = (total - high.astype(F32)).astype(BF16)
        convolved = matmul(back_high_ref[...], high) + (
            matmul(back_high_ref[...], low) + matmul(back_low_ref[...], high)
        )
        mixed = convolved + skip * block.astype(F32)
        out_refs[apart][...] = mixed.astype(BF16)


def mixed_pieces(part, tables, back_tables, skip, taps, partial, first, mine, across, beyond, ahead, after):
    members, chunk = taps.shape[1], taps.shape[-1]
    rows = tables[0].shape[1]
    return pl.pallas_call(
        functools.partial(mix_kernel, members, part),
        in_specs=[VMEM] * 12 + [pl.BlockSpec(memory_space=pl.ANY)],
        out_specs=[VMEM] * members,
        out_shape=[jax.ShapeDtypeStruct((rows, chunk), BF16)] * members,
        scratch_shapes=[
            pltpu.VMEM((members // 2, 2 * rows, chunk), F32),
            pltpu.VMEM((members, 2 * rows, chunk), F32),
        ],
        compiler_params=params(20),
        cost_estimate=SMALL,
    )(*tables, *back_tables, skip, taps, partial, first, mine, across, beyond, ahead, after)


def gate_kernel(layers, members, part, gate_ref, *refs):
    piece_refs, (out_hbm, out, sems) = refs[:members], refs[-3:]
    member, _ = place(members)
    count = sems.shape[0]
    step, wide = out.shape[0] // count, out.shape[1]
    here = slice(part * wide, (part + 1) * wide)
    copies = []
    for index in range(count):
        rows = slice(index * step, (index + 1) * step)
        for which, apart in enumerate(GATE_ORDER):
            held = member ^ apart
            for layer in range(layers):
                lanes = aligned(layer * members + held, LANES)
                source = aligned((part * layers + layer) * members + held, LANES)
                mixed = piece_refs[which][rows, layer * LANES : (layer + 1) * LANES].astype(F32)
                out[rows, lanes] = (gate_ref[rows, source].astype(F32) * mixed).astype(BF16)
        copies.append(pltpu.make_async_copy(out.at[rows], out_hbm.at[rows, here], sems.at[index]))
        copies[-1].start()
    for copy in copies:
        copy.wait()


def gated_output(part, gate_out, pieces, layers, members, out):
    rows, channels = gate_out.shape
    chunk = channels // members // CHUNKS
    width = channels // (layers * members)
    wide = channels // CHUNKS
    if width != LANES:
        member, _ = place(members)
        stacked = jnp.stack(pieces)
        stacked = jnp.stack(
            [lax.dynamic_index_in_dim(stacked, member ^ d, 0, False) for d in range(members)]
        )
        mixed = stacked.reshape(members, rows, layers // CHUNKS, width).transpose(1, 2, 0, 3)
        gate = gate_out[:, part * wide : (part + 1) * wide].astype(F32)
        gated = (gate * mixed.reshape(rows, wide).astype(F32)).astype(BF16)
        return gated if out is None else jnp.concatenate([out, gated], axis=1)
    more = [] if out is None else [out]
    count = 2
    return pl.pallas_call(
        functools.partial(gate_kernel, layers // CHUNKS, members, part),
        in_specs=[VMEM] * (1 + members) + [pl.BlockSpec(memory_space=pl.ANY)] * len(more),
        out_specs=pl.BlockSpec(memory_space=pl.ANY),
        out_shape=jax.ShapeDtypeStruct((rows, channels), BF16),
        scratch_shapes=[pltpu.VMEM((rows, wide), BF16), pltpu.SemaphoreType.DMA((count,))],
        input_output_aliases={members + 1: 0} if more else {},
        compiler_params=params(8),
        cost_estimate=SMALL,
    )(gate_out, *(pieces[apart] for apart in GATE_ORDER), *more)


def on_device(gate_out, gate_in, values, filter_taps, skip_gain):
    rows, channels = values.shape
    length = lax.axis_size("ctx")
    members = filter_taps.shape[0] // rows
    layers = length // members
    width = channels // length
    member, _ = place(members)
    tables, back_tables = forward_tables(rows), inverse_tables(rows)

    def to_member(value, apart, ahead):
        pairs = [
            (i, (i // members + ahead) % layers * members + (i % members ^ apart))
            for i in range(length)
        ]
        return lax.ppermute(value, "ctx", pairs)

    def to_layer(value, apart):
        pairs = [(i, (i // members ^ apart) * members + i % members) for i in range(length)]
        return lax.ppermute(value, "ctx", pairs)

    half = near_half(filter_taps, layers, lax.axis_size("groups"))
    near = one_away = None
    if half is not None:
        two_away, one_away = to_layer(half, 2), to_layer(half, 1)
    same, other, *send = product_pieces(gate_in, values, half, layers, members)
    if half is not None:
        one_away, send = lax.optimization_barrier((one_away, send))
    core = [to_member(piece, 1, 0) for piece in send]
    if half is not None:
        two_away, core = lax.optimization_barrier((two_away, core))
    mine, to_across, *to_beyond = payloads(same, other, core)
    if half is not None:
        three_away = to_layer(two_away, 1)
        near = joined([one_away, two_away, three_away])
    ahead = to_member(mine, 0, 1)
    beyond = [to_member(piece, 2, 1) for piece in to_beyond]
    across = to_member(to_across, 2, 0)
    taps = tap_spectra(tables, filter_taps, near, layers, members)
    partial, first, spectra = own_partials(tables, taps, mine, ahead, across)
    skip = skip_gain.reshape(1, channels)
    if width != LANES:
        skip = skip_gain.reshape(layers, members, width)
        skip = lax.dynamic_index_in_dim(skip, member, 1, False).reshape(CHUNKS, -1)
    out, after = None, first
    for part in range(CHUNKS):
        mixed = mixed_pieces(
            part, tables, back_tables, skip, taps, partial, first, mine, across, beyond[part], spectra, after
        )
        after = mixed[0]
        mixed = [mixed[0]] + [to_member(mixed[d], d, 0) for d in range(1, members)]
        out = gated_output(part, gate_out, mixed, layers, members, out)
    return out


def solution(mesh):
    in_specs = (
        P(("groups", "ctx"), None),
        P(("groups", "ctx"), None),
        P(("groups", "ctx"), None),
        P(None, "ctx"),
        P(),
    )
    out_specs = P(("groups", "ctx"), None)
    return jax.shard_map(
        on_device, mesh=mesh, in_specs=in_specs, out_specs=out_specs, check_vma=False
    )
```

```python
import functools

import jax
import jax.numpy as jnp
import ml_dtypes
import numpy as np
from jax import lax
from jax.experimental import pallas as pl
from jax.experimental.pallas import tpu as pltpu
from jax.sharding import PartitionSpec as P

LANES = 128
CHUNKS = 2
BF16 = jnp.bfloat16
F32 = jnp.float32
VMEM = pl.BlockSpec(memory_space=pltpu.VMEM)
GATE_ORDER = (0, 2, 3, 1)
SMALL = pl.CostEstimate(flops=1000, bytes_accessed=1000, transcendentals=0)


def two_parts(table):
    high = table.astype(ml_dtypes.bfloat16)
    low = (table - high.astype(np.float64)).astype(ml_dtypes.bfloat16)
    return jnp.asarray(high), jnp.asarray(low)


def bin_order(rows):
    return np.concatenate([np.arange(0, rows, 2), np.arange(1, rows, 2)])


def forward_tables(rows):
    bins = bin_order(rows)[:, None] + 0.5
    angle = bins * np.arange(rows)[None, :] * (np.pi / rows)
    return two_parts(np.concatenate([np.cos(angle), -np.sin(angle)], axis=0))


def inverse_tables(rows):
    bins = bin_order(rows)[None, :] + 0.5
    angle = bins * (np.arange(rows)[:, None] + rows) * (np.pi / rows)
    return two_parts(np.concatenate([np.cos(angle), -np.sin(angle)], axis=1) / rows)


def matmul(a, b):
    return jnp.dot(a, b, preferred_element_type=F32)


def params(mib):
    return pltpu.CompilerParams(vmem_limit_bytes=mib << 20)


def place(members):
    index = lax.axis_index("ctx")
    return lax.rem(index, members), lax.div(index, members)


def aligned(position, size):
    return pl.ds(pl.multiple_of(position * size, size), size)


def product_kernel(
    layers, members, gate_hbm, values_hbm, half_ref, keep_same_ref, keep_other_ref, *more
):
    del half_ref
    send_refs, (gate, values, sems) = more[:-3], more[-3:]
    member, _ = place(members)
    per_chunk = layers // CHUNKS
    count = sems.shape[1]
    step = gate.shape[0] // count

    def copies(index):
        rows = slice(index * step, (index + 1) * step)
        return [
            pltpu.make_async_copy(source.at[rows], target.at[rows], sems.at[which, index])
            for which, (source, target) in enumerate(((gate_hbm, gate), (values_hbm, values)))
        ]

    for index in range(count):
        for copy in copies(index):
            copy.start()
    refs = [
        lambda chunk, rows, lanes: keep_same_ref.at[chunk, rows, lanes],
        lambda chunk, rows, lanes: send_refs[2 * chunk].at[rows, lanes],
        lambda chunk, rows, lanes: keep_other_ref.at[chunk, rows, lanes],
        lambda chunk, rows, lanes: send_refs[2 * chunk + 1].at[rows, lanes],
    ]
    for index in range(count):
        rows = slice(index * step, (index + 1) * step)
        for copy in copies(index):
            copy.wait()
        for apart in range(members):
            held = member ^ apart
            for layer in range(layers):
                lanes = aligned(layer * members + held, LANES)
                gated = gate[rows, lanes].astype(F32) * values[rows, lanes].astype(F32)
                at = layer % per_chunk * LANES
                target = refs[apart](layer // per_chunk, rows, slice(at, at + LANES))
                target[...] = gated.astype(BF16)


def product_pieces(gate_in, values, half, layers, members):
    rows, channels = values.shape
    width = channels // (layers * members)
    chunk = channels // members // CHUNKS
    if width != LANES:
        member, _ = place(members)
        product = (gate_in.astype(F32) * values.astype(F32)).astype(BF16)
        product = product.reshape(rows, CHUNKS, layers // CHUNKS, members, width)
        product = product.transpose(3, 1, 0, 2, 4).reshape(members, CHUNKS, rows, chunk)
        pieces = [lax.dynamic_index_in_dim(product, member ^ d, 0, False) for d in range(members)]
        return pieces[0], pieces[2], pieces[1][0], pieces[3][0], pieces[1][1], pieces[3][1]
    count = 4
    there = pl.BlockSpec(memory_space=pltpu.HBM)
    return pl.pallas_call(
        functools.partial(product_kernel, layers, members),
        in_specs=[there, there, pl.BlockSpec(memory_space=pl.ANY)],
        out_specs=[VMEM] * (2 + 2 * CHUNKS),
        out_shape=[jax.ShapeDtypeStruct((CHUNKS, rows, chunk), BF16)] * 2
        + [jax.ShapeDtypeStruct((rows, chunk), BF16)] * (2 * CHUNKS),
        scratch_shapes=[pltpu.VMEM((rows, channels), BF16)] * 2 + [pltpu.SemaphoreType.DMA((2, count))],
        compiler_params=params(8),
        cost_estimate=SMALL,
    )(*(pltpu.with_memory_space_constraint(x, pltpu.HBM) for x in (gate_in, values)), half)


def pack_kernel(same_ref, other_ref, *refs):
    core_refs, (mine_ref, across_ref, *beyond_refs) = refs[: 2 * CHUNKS], refs[2 * CHUNKS :]
    for part in range(CHUNKS):
        mine_ref[part, 0] = same_ref[part]
        mine_ref[part, 1] = core_refs[2 * part][...]
        for target in (across_ref.at[part], beyond_refs[part]):
            target[0] = other_ref[part]
            target[1] = core_refs[2 * part + 1][...]


def payloads(same, other, core):
    _, rows, chunk = same.shape
    return pl.pallas_call(
        pack_kernel,
        in_specs=[VMEM] * (2 + len(core)),
        out_specs=[VMEM] * (2 + CHUNKS),
        out_shape=[jax.ShapeDtypeStruct((CHUNKS, 2, rows, chunk), BF16)] * 2
        + [jax.ShapeDtypeStruct((2, rows, chunk), BF16)] * CHUNKS,
        compiler_params=params(8),
        cost_estimate=SMALL,
    )(same, other, *core)


def join_kernel(*refs):
    at = 0
    for ref in refs[:-1]:
        count = ref.shape[0]
        refs[-1][at : at + count] = ref[...]
        at += count


def joined(pieces):
    return pl.pallas_call(
        join_kernel,
        in_specs=[VMEM] * len(pieces),
        out_specs=VMEM,
        out_shape=jax.ShapeDtypeStruct((sum(p.shape[0] for p in pieces), *pieces[0].shape[1:]), BF16),
        compiler_params=params(8),
        cost_estimate=SMALL,
    )(*pieces)


def put_tap_spectra(high_ref, low_ref, taps, out_ref):
    rows = high_ref.shape[1]
    chunk = out_ref.shape[-1]
    for part in range(CHUNKS):
        for lag in range(out_ref.shape[1]):
            block = taps[lag * rows : (lag + 1) * rows, part * chunk : (part + 1) * chunk]
            out_ref[part, lag] = matmul(high_ref[...], block) + matmul(low_ref[...], block)


def taps_kernel(layers, members, high_ref, low_ref, own_ref, near_ref, far_ref, out_ref, taps):
    _, layer = place(members)
    group = lax.axis_index("groups")
    half = near_ref.shape[1]
    near, far = aligned(group, half), aligned(1 - group, half)
    taps[:, aligned(layer, LANES)] = own_ref[...]
    for apart in range(1, layers):
        lanes = aligned(layer ^ apart, LANES)
        taps[near, lanes] = near_ref[apart - 1]
        taps[far, lanes] = far_ref[apart - 1]
    put_tap_spectra(high_ref, low_ref, taps, out_ref)


def half_kernel(taps_hbm, half_ref, sem):
    half = half_ref.shape[1]
    rows = aligned(lax.axis_index("groups"), half)
    copy = pltpu.make_async_copy(taps_hbm.at[rows], half_ref.at[0], sem)
    copy.start()
    copy.wait()


def near_half(filter_taps, layers, groups):
    count, width = filter_taps.shape
    if width != LANES or groups != 2 or layers != 4:
        return None
    return pl.pallas_call(
        half_kernel,
        in_specs=[pl.BlockSpec(memory_space=pltpu.HBM)],
        out_specs=VMEM,
        out_shape=jax.ShapeDtypeStruct((1, count // 2, width), BF16),
        scratch_shapes=[pltpu.SemaphoreType.DMA],
        compiler_params=params(8),
        cost_estimate=SMALL,
    )(pltpu.with_memory_space_constraint(filter_taps, pltpu.HBM))


def tap_spectra(tables, filter_taps, near, layers, members):
    count, width = filter_taps.shape
    rows = tables[0].shape[1]
    held = width * layers
    out_shape = jax.ShapeDtypeStruct((CHUNKS, count // rows, 2 * rows, held // CHUNKS), F32)
    if near is None:
        ring = [[layer * members + member for layer in range(layers)] for member in range(members)]
        taps = lax.all_gather(filter_taps, "ctx", axis=1, tiled=True, axis_index_groups=ring)
        return pl.pallas_call(
            put_tap_spectra,
            in_specs=[VMEM] * 3,
            out_specs=VMEM,
            out_shape=out_shape,
            compiler_params=params(20),
            cost_estimate=SMALL,
        )(*tables, taps)
    far = lax.ppermute(near, "groups", [(0, 1), (1, 0)])
    return pl.pallas_call(
        functools.partial(taps_kernel, layers, members),
        in_specs=[VMEM] * 5,
        out_specs=VMEM,
        out_shape=out_shape,
        scratch_shapes=[pltpu.VMEM((count, held), BF16)],
        compiler_params=params(20),
        cost_estimate=SMALL,
    )(*tables, filter_taps, near, far)


def window(before, after, sign):
    (before_real, before_imag), (real, imag) = before, after
    if sign > 0:
        return before_real + imag, before_imag - real
    return before_real - imag, before_imag + real


def sum_products(pairs):
    real_sum = imag_sum = None
    for (tap_real, tap_imag), (real, imag) in pairs:
        real_part = tap_real * real - tap_imag * imag
        imag_part = tap_real * imag + tap_imag * real
        real_sum = real_part if real_sum is None else real_sum + real_part
        imag_sum = imag_part if imag_sum is None else imag_sum + imag_part
    return real_sum, imag_sum


def for_bins(rows, step, body):
    count = rows // (2 * step)
    for sign, first in ((1, 0), (-1, count)):

        @pl.loop(first, first + count)
        def _(index):
            body(pl.multiple_of(index * step, step), sign)


def reader(ref, rows, at, step):
    def read(*index):
        return ref[*index, pl.ds(at, step), :], ref[*index, pl.ds(at + rows, step), :]

    return read


def own_kernel(
    members, high_ref, low_ref, taps_ref, mine_ref, ahead_ref, across_ref, part_ref, first_ref, halo_ref, spectra
):
    member, _ = place(members)
    rows = high_ref.shape[1]
    for part in range(CHUNKS):
        blocks = [mine_ref[part, 0], mine_ref[part, 1], across_ref[part, 0], across_ref[part, 1]]
        for apart, block in enumerate(blocks):
            spectra[member ^ apart] = matmul(high_ref[...], block) + matmul(low_ref[...], block)
        first_ref[part] = spectra[0]
        for apart in range(2):
            block = ahead_ref[part, apart]
            halo_ref[part, (member ^ apart) % 2] = matmul(high_ref[...], block) + matmul(low_ref[...], block)

        def body(at, sign):
            read = reader(spectra, rows, at, 8)
            taps_read = reader(taps_ref, rows, at, 8)
            taps = [taps_read(part, lag) for lag in range(members - 1)]
            blocks = [read(position) for position in range(members)]
            windows = [window(a, b, sign) for a, b in zip(blocks, blocks[1:])]
            for output in range(1, members):
                total = sum_products([(taps[lag], windows[output - 1 - lag]) for lag in range(output)])
                part_ref[part, output - 1, pl.ds(at, 8), :] = total[0]
                part_ref[part, output - 1, pl.ds(at + rows, 8), :] = total[1]

        for_bins(rows, 8, body)


def own_partials(tables, taps, *blocks):
    members = taps.shape[1]
    chunk = taps.shape[-1]
    rows = tables[0].shape[1]
    return pl.pallas_call(
        functools.partial(own_kernel, members),
        in_specs=[VMEM] * 6,
        out_specs=[VMEM] * 3,
        out_shape=[
            jax.ShapeDtypeStruct((CHUNKS, members - 1, 2 * rows, chunk), F32),
            jax.ShapeDtypeStruct((CHUNKS, 2 * rows, chunk), F32),
            jax.ShapeDtypeStruct((CHUNKS, members // 2, 2 * rows, chunk), F32),
        ],
        scratch_shapes=[pltpu.VMEM((members, 2 * rows, chunk), F32)],
        compiler_params=params(20),
        cost_estimate=SMALL,
    )(*tables, taps, *blocks)


def mix_kernel(
    members,
    part,
    high_ref,
    low_ref,
    back_high_ref,
    back_low_ref,
    skip_ref,
    taps_ref,
    part_ref,
    first_ref,
    mine_ref,
    across_ref,
    beyond_ref,
    ahead_ref,
    _,
    *refs,
):
    out_refs, (beyond, sums) = refs[:members], refs[members:]

    def skip_of(part):
        chunk = out_refs[0].shape[1]
        if skip_ref.shape[1] == chunk:
            return skip_ref[pl.ds(part, 1), :]
        shares = skip_ref.shape[1] // (members * LANES) // CHUNKS
        picked = [
            skip_ref[:, aligned((part * shares + layer) * members + member, LANES)]
            for layer in range(shares)
        ]
        return jnp.concatenate(picked, axis=1)

    member, _ = place(members)
    rows = high_ref.shape[1]
    for apart in range(2, members):
        block = beyond_ref[apart - 2]
        beyond[(member ^ apart) % 2] = matmul(high_ref[...], block) + matmul(low_ref[...], block)

    def body(pair, at, sign):
        halves = [reader(beyond, rows, at, 16)] * (members // 2)
        halves[pair] = functools.partial(reader(ahead_ref, rows, at, 16), part)
        taps_read = reader(taps_ref, rows, at, 16)
        taps = [taps_read(part, lag) for lag in range(members)]
        blocks = [halves[position // 2](position % 2) for position in range(members)]
        blocks.append(reader(first_ref, rows, at, 16)(part))
        windows = [window(a, b, sign) for a, b in zip(blocks, blocks[1:])]
        for output in range(members):
            total = sum_products(
                [(taps[lag], windows[members - 1 + output - lag]) for lag in range(output, members)]
            )
            if output:
                before = reader(part_ref, rows, at, 16)(part, output - 1)
                total = total[0] + before[0], total[1] + before[1]
            sums[output, pl.ds(at, 16), :] = total[0]
            sums[output, pl.ds(at + rows, 16), :] = total[1]

    for pair in range(members // 2):
        pl.when(member // 2 == pair)(
            functools.partial(for_bins, rows, 16, functools.partial(body, pair))
        )
    blocks = [mine_ref[part, 0], mine_ref[part, 1], across_ref[part, 0], across_ref[part, 1]]
    skip = skip_of(part)
    for apart, block in enumerate(blocks):
        total = sums[member ^ apart]
        high = total.astype(BF16)
        low = (total - high.astype(F32)).astype(BF16)
        convolved = matmul(back_high_ref[...], high) + (
            matmul(back_high_ref[...], low) + matmul(back_low_ref[...], high)
        )
        mixed = convolved + skip * block.astype(F32)
        out_refs[apart][...] = mixed.astype(BF16)


def mixed_pieces(part, tables, back_tables, skip, taps, partial, first, mine, across, beyond, ahead, after):
    members, chunk = taps.shape[1], taps.shape[-1]
    rows = tables[0].shape[1]
    return pl.pallas_call(
        functools.partial(mix_kernel, members, part),
        in_specs=[VMEM] * 12 + [pl.BlockSpec(memory_space=pl.ANY)],
        out_specs=[VMEM] * members,
        out_shape=[jax.ShapeDtypeStruct((rows, chunk), BF16)] * members,
        scratch_shapes=[
            pltpu.VMEM((members // 2, 2 * rows, chunk), F32),
            pltpu.VMEM((members, 2 * rows, chunk), F32),
        ],
        compiler_params=params(20),
        cost_estimate=SMALL,
    )(*tables, *back_tables, skip, taps, partial, first, mine, across, beyond, ahead, after)


def gate_kernel(layers, members, part, gate_ref, *refs):
    piece_refs, (out_hbm, out, sems) = refs[:members], refs[-3:]
    member, _ = place(members)
    count = sems.shape[0]
    step, wide = out.shape[0] // count, out.shape[1]
    here = slice(part * wide, (part + 1) * wide)
    copies = []
    for index in range(count):
        rows = slice(index * step, (index + 1) * step)
        for which, apart in enumerate(GATE_ORDER):
            held = member ^ apart
            for layer in range(layers):
                lanes = aligned(layer * members + held, LANES)
                source = aligned((part * layers + layer) * members + held, LANES)
                mixed = piece_refs[which][rows, layer * LANES : (layer + 1) * LANES].astype(F32)
                out[rows, lanes] = (gate_ref[rows, source].astype(F32) * mixed).astype(BF16)
        copies.append(pltpu.make_async_copy(out.at[rows], out_hbm.at[rows, here], sems.at[index]))
        copies[-1].start()
    for copy in copies:
        copy.wait()


def gated_output(part, gate_out, pieces, layers, members, out):
    rows, channels = gate_out.shape
    chunk = channels // members // CHUNKS
    width = channels // (layers * members)
    wide = channels // CHUNKS
    if width != LANES:
        member, _ = place(members)
        stacked = jnp.stack(pieces)
        stacked = jnp.stack(
            [lax.dynamic_index_in_dim(stacked, member ^ d, 0, False) for d in range(members)]
        )
        mixed = stacked.reshape(members, rows, layers // CHUNKS, width).transpose(1, 2, 0, 3)
        gate = gate_out[:, part * wide : (part + 1) * wide].astype(F32)
        gated = (gate * mixed.reshape(rows, wide).astype(F32)).astype(BF16)
        return gated if out is None else jnp.concatenate([out, gated], axis=1)
    more = [] if out is None else [out]
    count = 2
    return pl.pallas_call(
        functools.partial(gate_kernel, layers // CHUNKS, members, part),
        in_specs=[VMEM] * (1 + members) + [pl.BlockSpec(memory_space=pl.ANY)] * len(more),
        out_specs=pl.BlockSpec(memory_space=pl.ANY),
        out_shape=jax.ShapeDtypeStruct((rows, channels), BF16),
        scratch_shapes=[pltpu.VMEM((rows, wide), BF16), pltpu.SemaphoreType.DMA((count,))],
        input_output_aliases={members + 1: 0} if more else {},
        compiler_params=params(8),
        cost_estimate=SMALL,
    )(gate_out, *(pieces[apart] for apart in GATE_ORDER), *more)


def on_device(gate_out, gate_in, values, filter_taps, skip_gain):
    rows, channels = values.shape
    length = lax.axis_size("ctx")
    members = filter_taps.shape[0] // rows
    layers = length // members
    width = channels // length
    member, _ = place(members)
    tables, back_tables = forward_tables(rows), inverse_tables(rows)

    def to_member(value, apart, ahead):
        pairs = [
            (i, (i // members + ahead) % layers * members + (i % members ^ apart))
            for i in range(length)
        ]
        return lax.ppermute(value, "ctx", pairs)

    def to_layer(value, apart):
        pairs = [(i, (i // members ^ apart) * members + i % members) for i in range(length)]
        return lax.ppermute(value, "ctx", pairs)

    half = near_half(filter_taps, layers, lax.axis_size("groups"))
    near = one_away = None
    if half is not None:
        two_away, one_away = to_layer(half, 2), to_layer(half, 1)
    same, other, *send = product_pieces(gate_in, values, half, layers, members)
    if half is not None:
        one_away, send = lax.optimization_barrier((one_away, send))
    core = [to_member(piece, 1, 0) for piece in send]
    if half is not None:
        two_away, core = lax.optimization_barrier((two_away, core))
    mine, to_across, *to_beyond = payloads(same, other, core)
    if half is not None:
        three_away = to_layer(two_away, 1)
        near = joined([one_away, two_away, three_away])
    ahead = to_member(mine, 0, 1)
    beyond = [to_member(piece, 2, 1) for piece in to_beyond]
    across = to_member(to_across, 2, 0)
    taps = tap_spectra(tables, filter_taps, near, layers, members)
    partial, first, spectra = own_partials(tables, taps, mine, ahead, across)
    skip = skip_gain.reshape(1, channels)
    if width != LANES:
        skip = skip_gain.reshape(layers, members, width)
        skip = lax.dynamic_index_in_dim(skip, member, 1, False).reshape(CHUNKS, -1)
    out, after = None, first
    for part in range(CHUNKS):
        mixed = mixed_pieces(
            part, tables, back_tables, skip, taps, partial, first, mine, across, beyond[part], spectra, after
        )
        after = mixed[0]
        mixed = [mixed[0]] + [to_member(mixed[d], d, 0) for d in range(1, members)]
        out = gated_output(part, gate_out, mixed, layers, members, out)
    return out


def solution(mesh):
    in_specs = (
        P(("groups", "ctx"), None),
        P(("groups", "ctx"), None),
        P(("groups", "ctx"), None),
        P(None, "ctx"),
        P(),
    )
    out_specs = P(("groups", "ctx"), None)
    return jax.shard_map(
        on_device, mesh=mesh, in_specs=in_specs, out_specs=out_specs, check_vma=False
    )
```

```python
import functools

import jax
import jax.numpy as jnp
import ml_dtypes
import numpy as np
from jax import lax
from jax.experimental import pallas as pl
from jax.experimental.pallas import tpu as pltpu
from jax.sharding import PartitionSpec as P

LANES = 128
CHUNKS = 2
BF16 = jnp.bfloat16
F32 = jnp.float32
VMEM = pl.BlockSpec(memory_space=pltpu.VMEM)
GATE_ORDER = (0, 2, 3, 1)
SMALL = pl.CostEstimate(flops=1000, bytes_accessed=1000, transcendentals=0)


def two_parts(table):
    high = table.astype(ml_dtypes.bfloat16)
    low = (table - high.astype(np.float64)).astype(ml_dtypes.bfloat16)
    return jnp.asarray(high), jnp.asarray(low)


def bin_order(rows):
    return np.concatenate([np.arange(0, rows, 2), np.arange(1, rows, 2)])


def forward_tables(rows):
    bins = bin_order(rows)[:, None] + 0.5
    angle = bins * np.arange(rows)[None, :] * (np.pi / rows)
    return two_parts(np.concatenate([np.cos(angle), -np.sin(angle)], axis=0))


def inverse_tables(rows):
    bins = bin_order(rows)[None, :] + 0.5
    angle = bins * (np.arange(rows)[:, None] + rows) * (np.pi / rows)
    return two_parts(np.concatenate([np.cos(angle), -np.sin(angle)], axis=1) / rows)


def matmul(a, b):
    return jnp.dot(a, b, preferred_element_type=F32)


def params(mib):
    return pltpu.CompilerParams(vmem_limit_bytes=mib << 20)


def place(members):
    index = lax.axis_index("ctx")
    return lax.rem(index, members), lax.div(index, members)


def aligned(position, size):
    return pl.ds(pl.multiple_of(position * size, size), size)


def product_kernel(
    layers, members, gate_hbm, values_hbm, half_ref, keep_same_ref, keep_other_ref, *more
):
    del half_ref
    send_refs, (gate, values, sems) = more[:-3], more[-3:]
    member, _ = place(members)
    per_chunk = layers // CHUNKS
    count = sems.shape[1]
    step = gate.shape[0] // count

    def copies(index):
        rows = slice(index * step, (index + 1) * step)
        return [
            pltpu.make_async_copy(source.at[rows], target.at[rows], sems.at[which, index])
            for which, (source, target) in enumerate(((gate_hbm, gate), (values_hbm, values)))
        ]

    for index in range(count):
        for copy in copies(index):
            copy.start()
    refs = [
        lambda chunk, rows, lanes: keep_same_ref.at[chunk, rows, lanes],
        lambda chunk, rows, lanes: send_refs[2 * chunk].at[rows, lanes],
        lambda chunk, rows, lanes: keep_other_ref.at[chunk, rows, lanes],
        lambda chunk, rows, lanes: send_refs[2 * chunk + 1].at[rows, lanes],
    ]
    for index in range(count):
        rows = slice(index * step, (index + 1) * step)
        for copy in copies(index):
            copy.wait()
        for apart in range(members):
            held = member ^ apart
            for layer in range(layers):
                lanes = aligned(layer * members + held, LANES)
                gated = gate[rows, lanes].astype(F32) * values[rows, lanes].astype(F32)
                at = layer % per_chunk * LANES
                target = refs[apart](layer // per_chunk, rows, slice(at, at + LANES))
                target[...] = gated.astype(BF16)


def product_pieces(gate_in, values, half, layers, members):
    rows, channels = values.shape
    width = channels // (layers * members)
    chunk = channels // members // CHUNKS
    if width != LANES:
        member, _ = place(members)
        product = (gate_in.astype(F32) * values.astype(F32)).astype(BF16)
        product = product.reshape(rows, CHUNKS, layers // CHUNKS, members, width)
        product = product.transpose(3, 1, 0, 2, 4).reshape(members, CHUNKS, rows, chunk)
        pieces = [lax.dynamic_index_in_dim(product, member ^ d, 0, False) for d in range(members)]
        return pieces[0], pieces[2], pieces[1][0], pieces[3][0], pieces[1][1], pieces[3][1]
    count = 4
    there = pl.BlockSpec(memory_space=pltpu.HBM)
    return pl.pallas_call(
        functools.partial(product_kernel, layers, members),
        in_specs=[there, there, pl.BlockSpec(memory_space=pl.ANY)],
        out_specs=[VMEM] * (2 + 2 * CHUNKS),
        out_shape=[jax.ShapeDtypeStruct((CHUNKS, rows, chunk), BF16)] * 2
        + [jax.ShapeDtypeStruct((rows, chunk), BF16)] * (2 * CHUNKS),
        scratch_shapes=[pltpu.VMEM((rows, channels), BF16)] * 2 + [pltpu.SemaphoreType.DMA((2, count))],
        compiler_params=params(8),
        cost_estimate=SMALL,
    )(*(pltpu.with_memory_space_constraint(x, pltpu.HBM) for x in (gate_in, values)), half)


def pack_kernel(same_ref, other_ref, *refs):
    core_refs, (mine_ref, across_ref, *beyond_refs) = refs[: 2 * CHUNKS], refs[2 * CHUNKS :]
    for part in range(CHUNKS):
        mine_ref[part, 0] = same_ref[part]
        mine_ref[part, 1] = core_refs[2 * part][...]
        for target in (across_ref.at[part], beyond_refs[part]):
            target[0] = other_ref[part]
            target[1] = core_refs[2 * part + 1][...]


def payloads(same, other, core):
    _, rows, chunk = same.shape
    return pl.pallas_call(
        pack_kernel,
        in_specs=[VMEM] * (2 + len(core)),
        out_specs=[VMEM] * (2 + CHUNKS),
        out_shape=[jax.ShapeDtypeStruct((CHUNKS, 2, rows, chunk), BF16)] * 2
        + [jax.ShapeDtypeStruct((2, rows, chunk), BF16)] * CHUNKS,
        compiler_params=params(8),
        cost_estimate=SMALL,
    )(same, other, *core)


def join_kernel(*refs):
    at = 0
    for ref in refs[:-1]:
        count = ref.shape[0]
        refs[-1][at : at + count] = ref[...]
        at += count


def joined(pieces):
    return pl.pallas_call(
        join_kernel,
        in_specs=[VMEM] * len(pieces),
        out_specs=VMEM,
        out_shape=jax.ShapeDtypeStruct((sum(p.shape[0] for p in pieces), *pieces[0].shape[1:]), BF16),
        compiler_params=params(8),
        cost_estimate=SMALL,
    )(*pieces)


def put_tap_spectra(high_ref, low_ref, taps, out_ref):
    rows = high_ref.shape[1]
    chunk = out_ref.shape[-1]
    for part in range(CHUNKS):
        for lag in range(out_ref.shape[1]):
            block = taps[lag * rows : (lag + 1) * rows, part * chunk : (part + 1) * chunk]
            out_ref[part, lag] = matmul(high_ref[...], block) + matmul(low_ref[...], block)


def taps_kernel(layers, members, high_ref, low_ref, own_ref, near_ref, far_ref, out_ref, taps):
    _, layer = place(members)
    group = lax.axis_index("groups")
    half = near_ref.shape[1]
    near, far = aligned(group, half), aligned(1 - group, half)
    taps[:, aligned(layer, LANES)] = own_ref[...]
    for apart in range(1, layers):
        lanes = aligned(layer ^ apart, LANES)
        taps[near, lanes] = near_ref[apart - 1]
        taps[far, lanes] = far_ref[apart - 1]
    put_tap_spectra(high_ref, low_ref, taps, out_ref)


def half_kernel(taps_hbm, half_ref, sem):
    half = half_ref.shape[1]
    rows = aligned(lax.axis_index("groups"), half)
    copy = pltpu.make_async_copy(taps_hbm.at[rows], half_ref.at[0], sem)
    copy.start()
    copy.wait()


def near_half(filter_taps, layers, groups):
    count, width = filter_taps.shape
    if width != LANES or groups != 2 or layers != 4:
        return None
    return pl.pallas_call(
        half_kernel,
        in_specs=[pl.BlockSpec(memory_space=pltpu.HBM)],
        out_specs=VMEM,
        out_shape=jax.ShapeDtypeStruct((1, count // 2, width), BF16),
        scratch_shapes=[pltpu.SemaphoreType.DMA],
        compiler_params=params(8),
        cost_estimate=SMALL,
    )(pltpu.with_memory_space_constraint(filter_taps, pltpu.HBM))


def tap_spectra(tables, filter_taps, near, layers, members):
    count, width = filter_taps.shape
    rows = tables[0].shape[1]
    held = width * layers
    out_shape = jax.ShapeDtypeStruct((CHUNKS, count // rows, 2 * rows, held // CHUNKS), F32)
    if near is None:
        ring = [[layer * members + member for layer in range(layers)] for member in range(members)]
        taps = lax.all_gather(filter_taps, "ctx", axis=1, tiled=True, axis_index_groups=ring)
        return pl.pallas_call(
            put_tap_spectra,
            in_specs=[VMEM] * 3,
            out_specs=VMEM,
            out_shape=out_shape,
            compiler_params=params(20),
            cost_estimate=SMALL,
        )(*tables, taps)
    far = lax.ppermute(near, "groups", [(0, 1), (1, 0)])
    return pl.pallas_call(
        functools.partial(taps_kernel, layers, members),
        in_specs=[VMEM] * 5,
        out_specs=VMEM,
        out_shape=out_shape,
        scratch_shapes=[pltpu.VMEM((count, held), BF16)],
        compiler_params=params(20),
        cost_estimate=SMALL,
    )(*tables, filter_taps, near, far)


def window(before, after, sign):
    (before_real, before_imag), (real, imag) = before, after
    if sign > 0:
        return before_real + imag, before_imag - real
    return before_real - imag, before_imag + real


def sum_products(pairs):
    real_sum = imag_sum = None
    for (tap_real, tap_imag), (real, imag) in pairs:
        real_part = tap_real * real - tap_imag * imag
        imag_part = tap_real * imag + tap_imag * real
        real_sum = real_part if real_sum is None else real_sum + real_part
        imag_sum = imag_part if imag_sum is None else imag_sum + imag_part
    return real_sum, imag_sum


def for_bins(rows, step, body):
    count = rows // (2 * step)
    for sign, first in ((1, 0), (-1, count)):

        @pl.loop(first, first + count)
        def _(index):
            body(pl.multiple_of(index * step, step), sign)


def reader(ref, rows, at, step):
    def read(*index):
        return ref[*index, pl.ds(at, step), :], ref[*index, pl.ds(at + rows, step), :]

    return read


def own_kernel(
    members, high_ref, low_ref, taps_ref, mine_ref, ahead_ref, across_ref, part_ref, first_ref, halo_ref, spectra
):
    member, _ = place(members)
    rows = high_ref.shape[1]
    for part in range(CHUNKS):
        blocks = [mine_ref[part, 0], mine_ref[part, 1], across_ref[part, 0], across_ref[part, 1]]
        for apart, block in enumerate(blocks):
            spectra[member ^ apart] = matmul(high_ref[...], block) + matmul(low_ref[...], block)
        first_ref[part] = spectra[0]
        for apart in range(2):
            block = ahead_ref[part, apart]
            halo_ref[part, (member ^ apart) % 2] = matmul(high_ref[...], block) + matmul(low_ref[...], block)

        def body(at, sign):
            read = reader(spectra, rows, at, 8)
            taps_read = reader(taps_ref, rows, at, 8)
            taps = [taps_read(part, lag) for lag in range(members - 1)]
            blocks = [read(position) for position in range(members)]
            windows = [window(a, b, sign) for a, b in zip(blocks, blocks[1:])]
            for output in range(1, members):
                total = sum_products([(taps[lag], windows[output - 1 - lag]) for lag in range(output)])
                part_ref[part, output - 1, pl.ds(at, 8), :] = total[0]
                part_ref[part, output - 1, pl.ds(at + rows, 8), :] = total[1]

        for_bins(rows, 8, body)


def own_partials(tables, taps, *blocks):
    members = taps.shape[1]
    chunk = taps.shape[-1]
    rows = tables[0].shape[1]
    return pl.pallas_call(
        functools.partial(own_kernel, members),
        in_specs=[VMEM] * 6,
        out_specs=[VMEM] * 3,
        out_shape=[
            jax.ShapeDtypeStruct((CHUNKS, members - 1, 2 * rows, chunk), F32),
            jax.ShapeDtypeStruct((CHUNKS, 2 * rows, chunk), F32),
            jax.ShapeDtypeStruct((CHUNKS, members // 2, 2 * rows, chunk), F32),
        ],
        scratch_shapes=[pltpu.VMEM((members, 2 * rows, chunk), F32)],
        compiler_params=params(20),
        cost_estimate=SMALL,
    )(*tables, taps, *blocks)


def mix_kernel(
    members,
    part,
    high_ref,
    low_ref,
    back_high_ref,
    back_low_ref,
    skip_ref,
    taps_ref,
    part_ref,
    first_ref,
    mine_ref,
    across_ref,
    beyond_ref,
    ahead_ref,
    _,
    *refs,
):
    out_refs, (beyond, sums) = refs[:members], refs[members:]

    def skip_of(part):
        chunk = out_refs[0].shape[1]
        if skip_ref.shape[1] == chunk:
            return skip_ref[pl.ds(part, 1), :]
        shares = skip_ref.shape[1] // (members * LANES) // CHUNKS
        picked = [
            skip_ref[:, aligned((part * shares + layer) * members + member, LANES)]
            for layer in range(shares)
        ]
        return jnp.concatenate(picked, axis=1)

    member, _ = place(members)
    rows = high_ref.shape[1]
    for apart in range(2, members):
        block = beyond_ref[apart - 2]
        beyond[(member ^ apart) % 2] = matmul(high_ref[...], block) + matmul(low_ref[...], block)

    def body(pair, at, sign):
        halves = [reader(beyond, rows, at, 8)] * (members // 2)
        halves[pair] = functools.partial(reader(ahead_ref, rows, at, 8), part)
        taps_read = reader(taps_ref, rows, at, 8)
        taps = [taps_read(part, lag) for lag in range(members)]
        blocks = [halves[position // 2](position % 2) for position in range(members)]
        blocks.append(reader(first_ref, rows, at, 8)(part))
        windows = [window(a, b, sign) for a, b in zip(blocks, blocks[1:])]
        for output in range(members):
            total = sum_products(
                [(taps[lag], windows[members - 1 + output - lag]) for lag in range(output, members)]
            )
            if output:
                before = reader(part_ref, rows, at, 8)(part, output - 1)
                total = total[0] + before[0], total[1] + before[1]
            sums[output, pl.ds(at, 8), :] = total[0]
            sums[output, pl.ds(at + rows, 8), :] = total[1]

    for pair in range(members // 2):
        pl.when(member // 2 == pair)(
            functools.partial(for_bins, rows, 8, functools.partial(body, pair))
        )
    blocks = [mine_ref[part, 0], mine_ref[part, 1], across_ref[part, 0], across_ref[part, 1]]
    skip = skip_of(part)
    for apart, block in enumerate(blocks):
        total = sums[member ^ apart]
        total = total.astype(BF16)
        convolved = matmul(back_high_ref[...], total) + matmul(back_low_ref[...], total)
        mixed = convolved + skip * block.astype(F32)
        out_refs[apart][...] = mixed.astype(BF16)


def mixed_pieces(part, tables, back_tables, skip, taps, partial, first, mine, across, beyond, ahead, after):
    members, chunk = taps.shape[1], taps.shape[-1]
    rows = tables[0].shape[1]
    return pl.pallas_call(
        functools.partial(mix_kernel, members, part),
        in_specs=[VMEM] * 12 + [pl.BlockSpec(memory_space=pl.ANY)],
        out_specs=[VMEM] * members,
        out_shape=[jax.ShapeDtypeStruct((rows, chunk), BF16)] * members,
        scratch_shapes=[
            pltpu.VMEM((members // 2, 2 * rows, chunk), F32),
            pltpu.VMEM((members, 2 * rows, chunk), F32),
        ],
        compiler_params=params(20),
        cost_estimate=SMALL,
    )(*tables, *back_tables, skip, taps, partial, first, mine, across, beyond, ahead, after)


def gate_kernel(layers, members, part, gate_ref, *refs):
    piece_refs, (out_hbm, out, sems) = refs[:members], refs[-3:]
    member, _ = place(members)
    count = sems.shape[0]
    step, wide = out.shape[0] // count, out.shape[1]
    here = slice(part * wide, (part + 1) * wide)
    copies = []
    for index in range(count):
        rows = slice(index * step, (index + 1) * step)
        for which, apart in enumerate(GATE_ORDER):
            held = member ^ apart
            for layer in range(layers):
                lanes = aligned(layer * members + held, LANES)
                source = aligned((part * layers + layer) * members + held, LANES)
                mixed = piece_refs[which][rows, layer * LANES : (layer + 1) * LANES].astype(F32)
                out[rows, lanes] = (gate_ref[rows, source].astype(F32) * mixed).astype(BF16)
        copies.append(pltpu.make_async_copy(out.at[rows], out_hbm.at[rows, here], sems.at[index]))
        copies[-1].start()
    for copy in copies:
        copy.wait()


def gated_output(part, gate_out, pieces, layers, members, out):
    rows, channels = gate_out.shape
    chunk = channels // members // CHUNKS
    width = channels // (layers * members)
    wide = channels // CHUNKS
    if width != LANES:
        member, _ = place(members)
        stacked = jnp.stack(pieces)
        stacked = jnp.stack(
            [lax.dynamic_index_in_dim(stacked, member ^ d, 0, False) for d in range(members)]
        )
        mixed = stacked.reshape(members, rows, layers // CHUNKS, width).transpose(1, 2, 0, 3)
        gate = gate_out[:, part * wide : (part + 1) * wide].astype(F32)
        gated = (gate * mixed.reshape(rows, wide).astype(F32)).astype(BF16)
        return gated if out is None else jnp.concatenate([out, gated], axis=1)
    more = [] if out is None else [out]
    count = 2
    return pl.pallas_call(
        functools.partial(gate_kernel, layers // CHUNKS, members, part),
        in_specs=[VMEM] * (1 + members) + [pl.BlockSpec(memory_space=pl.ANY)] * len(more),
        out_specs=pl.BlockSpec(memory_space=pl.ANY),
        out_shape=jax.ShapeDtypeStruct((rows, channels), BF16),
        scratch_shapes=[pltpu.VMEM((rows, wide), BF16), pltpu.SemaphoreType.DMA((count,))],
        input_output_aliases={members + 1: 0} if more else {},
        compiler_params=params(8),
        cost_estimate=SMALL,
    )(gate_out, *(pieces[apart] for apart in GATE_ORDER), *more)


def on_device(gate_out, gate_in, values, filter_taps, skip_gain):
    rows, channels = values.shape
    length = lax.axis_size("ctx")
    members = filter_taps.shape[0] // rows
    layers = length // members
    width = channels // length
    member, _ = place(members)
    tables, back_tables = forward_tables(rows), inverse_tables(rows)

    def to_member(value, apart, ahead):
        pairs = [
            (i, (i // members + ahead) % layers * members + (i % members ^ apart))
            for i in range(length)
        ]
        return lax.ppermute(value, "ctx", pairs)

    def to_layer(value, apart):
        pairs = [(i, (i // members ^ apart) * members + i % members) for i in range(length)]
        return lax.ppermute(value, "ctx", pairs)

    half = near_half(filter_taps, layers, lax.axis_size("groups"))
    near = one_away = None
    if half is not None:
        two_away, one_away = to_layer(half, 2), to_layer(half, 1)
    same, other, *send = product_pieces(gate_in, values, half, layers, members)
    if half is not None:
        one_away, send = lax.optimization_barrier((one_away, send))
    core = [to_member(piece, 1, 0) for piece in send]
    if half is not None:
        two_away, core = lax.optimization_barrier((two_away, core))
    mine, to_across, *to_beyond = payloads(same, other, core)
    if half is not None:
        three_away = to_layer(two_away, 1)
        near = joined([one_away, two_away, three_away])
    ahead = to_member(mine, 0, 1)
    beyond = [to_member(piece, 2, 1) for piece in to_beyond]
    across = to_member(to_across, 2, 0)
    taps = tap_spectra(tables, filter_taps, near, layers, members)
    partial, first, spectra = own_partials(tables, taps, mine, ahead, across)
    skip = skip_gain.reshape(1, channels)
    if width != LANES:
        skip = skip_gain.reshape(layers, members, width)
        skip = lax.dynamic_index_in_dim(skip, member, 1, False).reshape(CHUNKS, -1)
    out, after = None, first
    for part in range(CHUNKS):
        mixed = mixed_pieces(
            part, tables, back_tables, skip, taps, partial, first, mine, across, beyond[part], spectra, after
        )
        after = mixed[0]
        mixed = [mixed[0]] + [to_member(mixed[d], d, 0) for d in range(1, members)]
        out = gated_output(part, gate_out, mixed, layers, members, out)
    return out


def solution(mesh):
    in_specs = (
        P(("groups", "ctx"), None),
        P(("groups", "ctx"), None),
        P(("groups", "ctx"), None),
        P(None, "ctx"),
        P(),
    )
    out_specs = P(("groups", "ctx"), None)
    return jax.shard_map(
        on_device, mesh=mesh, in_specs=in_specs, out_specs=out_specs, check_vma=False
    )
```
